32 devices in a mesh: sub: 16 (over z, y, core), strip: 2 (over x).
Axes of the slice: x: 2, y: 2, z: 4, core: 2. Of those that a mesh axis runs over, the one named last changes fastest.
Arguments:
- spectra: bfloat16 [32, 256, 2048], P('sub', 'strip'), may hold values from -6 to 6
- offsets: int32 [32], P('sub'), may hold values from 0 to 1023
Outputs:
- foreground: float32 [1024, 256, 32], P('strip', 'sub')
The draws below stay inside these ranges and needn't reach their ends.
All inputs are finite; a program needn't handle non-finite values.
Results may differ from the reference program's by a relative error of at most 0.0068.
Values may be sent and summed in bfloat16 or wider, within the bound.
A program may use at most 64 MiB of HBM per device.

```python
import math
import jax
import jax.numpy as jnp
from jax import lax

KR = 256
KA = 1024
ROWS = 1024
COLS = 256
WIN = 8
BG = 16
SUBAP = 32


def set_ends(entries, own_key, smallest, largest):
    longest = entries.shape.index(max(entries.shape))
    spots = []
    for shift in (0, 1):
        where = [jax.random.randint(jax.random.fold_in(own_key, axis), (), 0, length) for axis, length in enumerate(entries.shape)]
        where[longest] = (where[longest] + shift) % entries.shape[longest]
        spots.append(tuple(where))
    return entries.at[spots[0]].set(smallest).at[spots[1]].set(largest)


def steps_of(key, shape, pieces, low, largest):
    level, own = 1.0, jax.random.fold_in(key, 6)
    for axis_at, blocks in pieces:
        draws = jnp.exp(jax.random.uniform(jax.random.fold_in(own, axis_at), (blocks,), jnp.float32, low / len(pieces), largest / len(pieces)))
        level = level * jnp.repeat(draws, shape[axis_at] // blocks).reshape([-1 if axis == axis_at else 1 for axis in range(len(shape))])
    return level


def gaussian(stream_key, dims, scale, bound, cuts=(), held_as=jnp.bfloat16):
    result = jax.random.normal(stream_key, dims, jnp.float32) * scale
    if len(cuts) > 0:
        result = steps_of(stream_key, dims, cuts, -0.22, 0.18) * result
    return jnp.clip(result, min=-bound, max=bound).astype(held_as)


def setup_inputs(seed: int = 0) -> dict:
    keys = jax.random.split(jax.random.key(seed), 3)
    return {
        "spectra": gaussian(keys[0], (SUBAP, KR, 2 * KA), 1.0, 6.0, ((0, 16), (1, 2))),
        "offsets": set_ends(jax.random.randint(keys[1], (SUBAP,), 0, ROWS), jax.random.fold_in(keys[1], 1), 0, ROWS - 1).astype(jnp.int32),
    }


def column_table(samples, width):
    sample_index = jnp.arange(samples, dtype=jnp.int32)[:, None]
    column_index = jnp.arange(width, dtype=jnp.int32)[None, :]
    phase = jnp.mod(sample_index * column_index, samples).astype(jnp.float32) * (2.0 * math.pi / samples)
    cosine = jnp.cos(phase) / math.sqrt(samples)
    sine = -jnp.sin(phase) / math.sqrt(samples)
    upper = jnp.concatenate([cosine, sine], axis=1)
    lower = jnp.concatenate([-sine, cosine], axis=1)
    return jnp.concatenate([upper, lower], axis=0).astype(jnp.bfloat16)

def row_table(row_index, samples, image_rows):
    sample_index = jnp.arange(samples, dtype=jnp.int32)[None, :] - samples // 2
    phase = jnp.mod(row_index[:, None] * sample_index, image_rows).astype(jnp.float32) * (2.0 * math.pi / image_rows)
    scale = 1.0 / math.sqrt(samples)
    return jnp.concatenate([jnp.cos(phase) * scale, jnp.sin(phase) * scale], axis=0).astype(jnp.bfloat16)

def apply_phase(mixed, offset, sample_index, samples, image_rows, width):
    angle = jnp.mod(offset * (sample_index - samples // 2), image_rows).astype(jnp.float32) * (2.0 * math.pi / image_rows)
    cosine = jnp.cos(angle)[:, None]
    sine = jnp.sin(angle)[:, None]
    real_part = mixed[:, :width]
    imag_part = mixed[:, width:]
    return jnp.concatenate([real_part * cosine - imag_part * sine, real_part * sine + imag_part * cosine], axis=1).astype(jnp.bfloat16)

def reference(spectra, offsets):
    columns = column_table(KA, COLS)
    table = row_table(jnp.arange(ROWS, dtype=jnp.int32), KR, ROWS)
    samples_all = jnp.arange(KR, dtype=jnp.int32)

    def single(inputs):
        spectrum, offset = inputs
        mixed = jnp.dot(spectrum, columns, preferred_element_type=jnp.float32)
        shifted = apply_phase(mixed, offset, samples_all, KR, ROWS, COLS)
        product = jnp.dot(table, shifted, preferred_element_type=jnp.float32)
        real_part = product[:ROWS, :COLS] - product[ROWS:, COLS:]
        imag_part = product[:ROWS, COLS:] + product[ROWS:, :COLS]
        return jnp.concatenate([real_part, imag_part], axis=1)
    images = lax.map(single, (spectra, offsets))
    frames = images
    for lead in range(1, WIN):
        frames = frames + jnp.roll(images, -lead, axis=0)
    real_part = frames[:, :, :COLS]
    imag_part = frames[:, :, COLS:]
    log_power = jnp.log(1.0 + real_part * real_part + imag_part * imag_part)
    padded = jnp.pad(log_power, ((0, 0), (1, 1), (1, 1)))
    total = jnp.zeros_like(log_power)
    for row_step in range(3):
        for col_step in range(3):
            total = total + padded[:, row_step:row_step + ROWS, col_step:col_step + COLS]
    filtered = total / 9.0
    background = jnp.zeros_like(filtered)
    for behind in range(BG):
        background = background + jnp.roll(filtered, behind, axis=0)
    background = background / BG
    return jnp.transpose(filtered - background, (1, 2, 0))
```

```python
import math

import jax
import jax.numpy as jnp
import numpy as np
from jax import lax
from jax.sharding import PartitionSpec as P

KR = 256
ROWS = 1024
COLS = 256
WIN = 8
BG = 16


def column_table(samples, parts):
    wide = COLS // parts + 2
    column = (np.arange(parts) * (wide - 2))[:, None] + np.arange(-1, wide - 1)[None, :]
    inside = (column >= 0) & (column < COLS)
    phase = ((np.arange(samples)[:, None, None] * column[None]) % samples) * (2.0 * math.pi / samples)
    cosine = np.where(inside, np.cos(phase), 0.0) / math.sqrt(samples)
    sine = np.where(inside, -np.sin(phase), 0.0) / math.sqrt(samples)
    upper = np.stack([cosine, sine], axis=2)
    lower = np.stack([-sine, cosine], axis=2)
    return jnp.asarray(np.concatenate([upper, lower], axis=0).astype(np.float32)).astype(jnp.bfloat16)


def row_table(rows):
    sample = jnp.arange(KR, dtype=jnp.int32)[:, None] - KR // 2
    phase = jnp.mod(rows[None, :] * sample, ROWS).astype(jnp.float32) * (2.0 * math.pi / ROWS)
    scale = jnp.where((rows >= 0) & (rows < ROWS), 1.0 / math.sqrt(KR), 0.0)[None, :]
    cosine = jnp.cos(phase) * scale
    sine = jnp.sin(phase) * scale
    upper = jnp.stack([cosine, sine], axis=1)
    lower = jnp.stack([-sine, cosine], axis=1)
    return jnp.concatenate([upper, lower], axis=0).astype(jnp.bfloat16)


def rotation(offsets, samples):
    angle = jnp.mod(offsets[:, None] * (samples[None, :] - KR // 2), ROWS).astype(jnp.float32) * (2.0 * math.pi / ROWS)
    return jnp.cos(angle), jnp.sin(angle)


def plain_body(spectra, offsets):
    own, depth = spectra.shape[:2]
    parts, strips = lax.axis_size("sub"), lax.axis_size("strip")
    wide = COLS // parts + 2
    high = ROWS // strips
    strip = lax.axis_index("strip")
    frames = own * parts
    table = column_table(spectra.shape[2] // 2, parts)
    cosine, sine = rotation(offsets, strip * depth + jnp.arange(depth, dtype=jnp.int32))
    mixed = jnp.einsum("skc,cdpn->dspnk", spectra, table, preferred_element_type=jnp.float32)
    real, imag = mixed[:, :, 0], mixed[:, :, 1]
    cosine, sine = cosine[None, :, None, :], sine[None, :, None, :]
    shifted = jnp.stack([real * cosine - imag * sine, real * sine + imag * cosine], axis=2).astype(jnp.bfloat16)
    held = lax.all_to_all(shifted, "sub", split_axis=0, concat_axis=0, tiled=True)
    held = held.reshape(frames, 2, wide, depth)
    whole = jnp.zeros((frames, 2, wide, strips, depth), jnp.bfloat16)
    for step in range(strips):
        part = held
        if step:
            part = lax.ppermute(held, "strip", [(i, (i + step) % strips) for i in range(strips)])
        source = jnp.mod(strip - step, strips)
        whole = lax.dynamic_update_slice(whole, part[:, :, :, None], (0, 0, 0, source, 0))
    wider = whole.reshape(frames, 2, wide, KR).astype(jnp.float32)
    summed = wider
    for lead in range(1, WIN):
        summed = summed + jnp.roll(wider, -lead, axis=0)
    rows = strip * high + jnp.arange(-1, high + 1, dtype=jnp.int32)
    product = jnp.einsum(
        "fpnk,pkqm->qnfm",
        summed.astype(jnp.bfloat16),
        row_table(rows).reshape(2, KR, 2, high + 2),
        preferred_element_type=jnp.float32,
    )
    log_power = jnp.log(1.0 + product[0] * product[0] + product[1] * product[1])
    total = log_power[:, :, :-2] + log_power[:, :, 1:-1] + log_power[:, :, 2:]
    filtered = (total[:-2] + total[1:-1] + total[2:]) / 9.0
    background = filtered
    for behind in range(1, BG):
        background = background + jnp.roll(filtered, behind, axis=1)
    return jnp.transpose(filtered - background / BG, (2, 0, 1))


def solution(mesh):
    in_specs = (P("sub", "strip", None), P("sub"))
    out_specs = P("strip", "sub", None)
    return jax.shard_map(plain_body, mesh=mesh, in_specs=in_specs, out_specs=out_specs, check_vma=False)
```

```python
import functools
import math

import jax
import jax.numpy as jnp
import numpy as np
from jax import lax
from jax.experimental import pallas as pl
from jax.experimental.pallas import tpu as pltpu
from jax.sharding import PartitionSpec as P

KR = 256
ROWS = 1024
COLS = 256
WIN = 8
BG = 16


def column_table(samples, parts):
    wide = COLS // parts + 2
    column = (np.arange(parts) * (wide - 2))[:, None] + np.arange(-1, wide - 1)[None, :]
    inside = (column >= 0) & (column < COLS)
    phase = ((np.arange(samples)[:, None, None] * column[None]) % samples) * (2.0 * math.pi / samples)
    cosine = np.where(inside, np.cos(phase), 0.0) / math.sqrt(samples)
    sine = np.where(inside, -np.sin(phase), 0.0) / math.sqrt(samples)
    upper = np.stack([cosine, sine], axis=2)
    lower = np.stack([-sine, cosine], axis=2)
    return jnp.asarray(np.concatenate([upper, lower], axis=0).astype(np.float32)).astype(jnp.bfloat16)


def row_table(rows):
    sample = jnp.arange(KR, dtype=jnp.int32)[:, None] - KR // 2
    phase = jnp.mod(rows[None, :] * sample, ROWS).astype(jnp.float32) * (2.0 * math.pi / ROWS)
    scale = jnp.where((rows >= 0) & (rows < ROWS), 1.0 / math.sqrt(KR), 0.0)[None, :]
    cosine = jnp.cos(phase) * scale
    sine = jnp.sin(phase) * scale
    upper = jnp.stack([cosine, sine], axis=1)
    lower = jnp.stack([-sine, cosine], axis=1)
    return jnp.concatenate([upper, lower], axis=0).astype(jnp.bfloat16)


def rotation(offsets, samples):
    angle = jnp.mod(offsets[:, None] * (samples[None, :] - KR // 2), ROWS).astype(jnp.float32) * (2.0 * math.pi / ROWS)
    return jnp.cos(angle), jnp.sin(angle)


def plain_body(spectra, offsets):
    own, depth = spectra.shape[:2]
    parts, strips = lax.axis_size("sub"), lax.axis_size("strip")
    wide = COLS // parts + 2
    high = ROWS // strips
    strip = lax.axis_index("strip")
    frames = own * parts
    table = column_table(spectra.shape[2] // 2, parts)
    cosine, sine = rotation(offsets, strip * depth + jnp.arange(depth, dtype=jnp.int32))
    mixed = jnp.einsum("skc,cdpn->dspnk", spectra, table, preferred_element_type=jnp.float32)
    real, imag = mixed[:, :, 0], mixed[:, :, 1]
    cosine, sine = cosine[None, :, None, :], sine[None, :, None, :]
    shifted = jnp.stack([real * cosine - imag * sine, real * sine + imag * cosine], axis=2).astype(jnp.bfloat16)
    held = lax.all_to_all(shifted, "sub", split_axis=0, concat_axis=0, tiled=True)
    held = held.reshape(frames, 2, wide, depth)
    whole = jnp.zeros((frames, 2, wide, strips, depth), jnp.bfloat16)
    for step in range(strips):
        part = held
        if step:
            part = lax.ppermute(held, "strip", [(i, (i + step) % strips) for i in range(strips)])
        source = jnp.mod(strip - step, strips)
        whole = lax.dynamic_update_slice(whole, part[:, :, :, None], (0, 0, 0, source, 0))
    wider = whole.reshape(frames, 2, wide, KR).astype(jnp.float32)
    summed = wider
    for lead in range(1, WIN):
        summed = summed + jnp.roll(wider, -lead, axis=0)
    rows = strip * high + jnp.arange(-1, high + 1, dtype=jnp.int32)
    product = jnp.einsum(
        "fpnk,pkqm->qnfm",
        summed.astype(jnp.bfloat16),
        row_table(rows).reshape(2, KR, 2, high + 2),
        preferred_element_type=jnp.float32,
    )
    log_power = jnp.log(1.0 + product[0] * product[0] + product[1] * product[1])
    total = log_power[:, :, :-2] + log_power[:, :, 1:-1] + log_power[:, :, 2:]
    filtered = (total[:-2] + total[1:-1] + total[2:]) / 9.0
    background = filtered
    for behind in range(1, BG):
        background = background + jnp.roll(filtered, behind, axis=1)
    return jnp.transpose(filtered - background / BG, (2, 0, 1))


LANES = 128
MESH = pl.DeviceIdType.MESH


def column_planes(samples):
    phase = (np.arange(COLS)[:, None] * np.arange(samples)[None, :] % samples) * (2.0 * math.pi / samples)
    planes = np.stack([np.cos(phase), -np.sin(phase)]) / math.sqrt(samples)
    return jnp.asarray(planes.astype(np.float32).astype(jnp.bfloat16))


def row_planes(high):
    row = np.concatenate([np.arange(high + LANES - 1), [-1]])
    used = (row <= high)[None, :]
    sample = np.arange(KR)[:, None] - KR // 2
    phase = (row[None, :] * sample % ROWS) * (2.0 * math.pi / ROWS)
    planes = np.stack([np.cos(phase) * used, np.sin(phase) * used]) / math.sqrt(KR)
    return jnp.asarray(planes.astype(np.float32).astype(jnp.bfloat16))


def frame_weights(width, sources, rows):
    frames = 2 * sources
    weights = np.zeros((width, frames, rows), np.float32)
    target = np.arange(frames)

    def place(at, column, frame):
        series = np.where(target == frame, 1.0, 0.0) - np.where((target - frame) % frames < BG, 1.0 / BG, 0.0)
        for near in range(max(column - 1, 0), min(column + 2, width)):
            weights[near, :, at] = series

    for lane in range(2):
        for source in range(sources):
            frame = 2 * source + lane
            for column in range(width):
                place((lane * sources + source) * width + column, column, frame)
            for side in range(2):
                place(2 * sources * width + (lane * sources + source) * 2 + side, (-1, width)[side], frame)
    return jnp.asarray(weights.reshape(width * frames, rows).astype(jnp.bfloat16))


def send_order(count):
    order = []
    for away in range(count // 2, 0, -1):
        order += [away] if 2 * away == count else [away, count - away]
    return order


def product_of(a, b):
    return lax.dot_general(a, b, (((1,), (0,)), ((), ())), preferred_element_type=jnp.float32)


def product_t(a, b):
    return lax.dot_general(a, b, (((1,), (1,)), ((), ())), preferred_element_type=jnp.float32)


def ahead(value, steps):
    return jnp.concatenate([value[steps:], value[:steps]], axis=0)


def kernel(
    parts, strips, offsets_ref, spectra_hbm, columns_hbm, rows_hbm, weights_hbm, out_ref,
    spectra, columns, rows, weights, real, imag, edge, main, halo, held, held_halo, lhs, boxed, level,
    load_sem, own_sem, send_sem, recv_sem, pass_sem, got_sem,
):
    me, strip = lax.axis_index("sub"), lax.axis_index("strip")
    width = COLS // parts
    depth = spectra.shape[1]
    samples = spectra.shape[2] // 2
    high = out_ref.shape[2]
    other = 1 - strip

    loads = [
        pltpu.make_async_copy(source, target, load_sem.at[i])
        for i, (source, target) in enumerate(
            [(spectra_hbm, spectra), (columns_hbm, columns), (rows_hbm, rows), (weights_hbm, weights)]
        )
    ]
    for load in loads:
        load.start()
    barrier = pltpu.get_barrier_semaphore()
    for away in range(1, parts):
        pl.semaphore_signal(barrier, inc=1, device_id=(lax.rem(me + away, parts), strip), device_id_type=MESH)
    pl.semaphore_signal(barrier, inc=1, device_id=(me, other), device_id_type=MESH)

    lane = lax.broadcasted_iota(jnp.int32, (1, 2 * depth), 1)
    sample = strip * depth + jnp.where(lane < depth, lane, lane - depth) - KR // 2
    offset = jnp.where(lane < depth, offsets_ref[0], offsets_ref[1])
    angle = jnp.bitwise_and(offset * sample, ROWS - 1).astype(jnp.float32) * (2.0 * math.pi / ROWS)
    cosine, sine = jnp.cos(angle), jnp.sin(angle)
    edge[...] = jnp.zeros_like(edge)
    loads[0].wait()
    loads[1].wait()
    data = spectra[...].reshape(2 * depth, 2 * samples)
    data_re, data_im = data[:, :samples], data[:, samples:]
    step = 64
    for at in range(0, COLS, step):
        cos_part, sin_part = columns[0, at : at + step], columns[1, at : at + step]
        re = product_t(cos_part, data_re) - product_t(sin_part, data_im)
        im = product_t(sin_part, data_re) + product_t(cos_part, data_im)
        first = at // width
        for part, value, ref in ((0, re * cosine - im * sine, real), (1, re * sine + im * cosine, imag)):
            ref[at : at + step] = value
            blocks = value.reshape(step // width, width, 2 * depth).astype(jnp.bfloat16)
            for own in range(2):
                main[first : first + step // width, own * width : (own + 1) * width, part * depth : (part + 1) * depth] = (
                    blocks[:, :, own * depth : (own + 1) * depth]
                )
    for part, ref in ((0, real), (1, imag)):
        for own in range(2):
            lanes, into = slice(own * depth, (own + 1) * depth), slice(part * depth, (part + 1) * depth)
            for d in range(parts):
                if d > 0:
                    edge[d, 2 * own : 2 * own + 1, into] = ref[d * width - 1 : d * width, lanes]
                if d < parts - 1:
                    edge[d, 2 * own + 1 : 2 * own + 2, into] = ref[(d + 1) * width : (d + 1) * width + 1, lanes]
    halo[...] = edge[...].astype(jnp.bfloat16)

    pl.semaphore_wait(barrier, parts)

    def sends(to, where):
        return [
            pltpu.make_async_remote_copy(
                src_ref=source.at[to], dst_ref=target.at[strip, where], send_sem=send_sem.at[kind, to],
                recv_sem=recv_sem.at[kind, where], device_id=(to, strip), device_id_type=MESH,
            )
            for kind, source, target in ((0, main, held), (1, halo, held_halo))
        ]

    def passes(h, source, own=False):
        return [
            pltpu.make_async_remote_copy(
                src_ref=block.at[source] if own else target.at[h, source], dst_ref=target.at[h, source],
                send_sem=pass_sem.at[kind, source], recv_sem=got_sem.at[kind, source],
                device_id=(me, other), device_id_type=MESH,
            )
            for kind, block, target in ((0, main, held), (1, halo, held_halo))
        ]

    order = send_order(parts)
    for away in order:
        for copy in sends(lax.rem(me + away, parts), me):
            copy.start()
    kept = [
        pltpu.make_async_copy(source.at[me], target.at[strip, me], own_sem.at[kind])
        for kind, source, target in ((0, main, held), (1, halo, held_halo))
    ]
    for copy in passes(strip, me, own=True) + kept:
        copy.start()
    for away in reversed(order):
        source = lax.rem(me + parts - away, parts)
        for copy in sends(source, source):
            copy.wait_recv()
        for copy in passes(strip, source):
            copy.start()
    for copy in kept:
        copy.wait()
    for away in [0] + order[::-1]:
        for copy in passes(other, lax.rem(me + parts - away, parts)):
            copy.wait_recv()
    for away in order:
        for copy in sends(lax.rem(me + away, parts), me):
            copy.wait_send()
    for away in [0] + order:
        for copy in passes(strip, lax.rem(me + away, parts), own=away == 0):
            copy.wait_send()

    top = 2 * parts * width
    odd = lax.rem(lax.broadcasted_iota(jnp.int32, (1, 1, 2 * depth), 2), 2)
    sign = 1.0 - 2.0 * (odd * strip).astype(jnp.float32)
    row_at = lax.broadcasted_iota(jnp.int32, (parts, 8, 2 * depth), 1)
    for h in range(2):
        block = held[h].astype(jnp.float32) * sign
        first, second = block[:, :width], block[:, width:]
        near = held_halo[h].astype(jnp.float32) * sign
        near_second = jnp.concatenate([pltpu.roll(near[i], 6, 0)[None] for i in range(parts)], axis=0)
        for is_halo, one, two in ((False, first, second), (True, near, near_second)):
            pair = one + two
            double = pair + ahead(pair, 1)
            quad = double + ahead(double, 2)
            for own, frame in ((0, quad), (1, quad - one + ahead(one, WIN // 2))):
                if is_halo:
                    frame = jnp.where(row_at < 2, frame, 0.0)
                    packed = []
                    for group in range(parts // 4):
                        total = frame[4 * group]
                        for j in range(1, 4):
                            total = total + pltpu.roll(frame[4 * group + j], 2 * j, 0)
                        packed.append(total)
                    flat = jnp.concatenate(packed, axis=0).astype(jnp.bfloat16)
                    at, size = top + own * 2 * parts, 2 * parts
                else:
                    flat = frame.reshape(parts * width, 2 * depth).astype(jnp.bfloat16)
                    at, size = own * parts * width, parts * width
                for part in range(2):
                    lhs[at : at + size, part * KR + h * depth : part * KR + (h + 1) * depth] = flat[
                        :, part * depth : (part + 1) * depth
                    ]

    loads[2].wait()
    total_rows = top + 4 * parts
    tail = lax.broadcasted_iota(jnp.int32, (1, high + LANES), 1)
    outside = ((tail == high) & (strip == strips - 1)) | ((tail == high + LANES - 1) & (strip == 0))
    inside = jnp.where(outside, 0.0, 1.0)
    chunk = 64
    for at in range(0, total_rows, chunk):
        left_re, left_im = lhs[at : at + chunk, :KR], lhs[at : at + chunk, KR:]
        re = product_of(left_re, rows[0]) - product_of(left_im, rows[1])
        im = product_of(left_re, rows[1]) + product_of(left_im, rows[0])
        power = jnp.log(1.0 + re * re + im * im) * inside
        summed = power + pltpu.roll(power, 1, 1) + pltpu.roll(power, high + LANES - 1, 1)
        boxed[at : at + chunk] = summed[:, :high]

    frames = 2 * parts
    block = boxed[:top].reshape(frames, width, high)
    mean = jnp.sum(block, axis=0, keepdims=True) * (1.0 / frames)
    level[:top] = (block - mean).reshape(top, high).astype(jnp.bfloat16)
    near = boxed[top:total_rows].reshape(frames // 4, 8, high)
    mean = jnp.sum(near, axis=0) * (1.0 / frames)
    mean = mean + pltpu.roll(mean, 4, 0)
    mean = mean + pltpu.roll(mean, 2, 0)
    level[top:total_rows] = (near - mean[None]).reshape(total_rows - top, high).astype(jnp.bfloat16)
    level[total_rows:] = jnp.zeros((level.shape[0] - total_rows, high), jnp.bfloat16)
    loads[3].wait()
    for c in range(0, width, 4):
        piece = product_of(weights[c * frames : (c + 4) * frames], level[...])
        out_ref[c : c + 4] = (piece * (1.0 / 9.0)).reshape(4, frames, high)


def kernel_body(spectra, offsets):
    parts, strips = lax.axis_size("sub"), lax.axis_size("strip")
    own, depth, both = spectra.shape
    width, high = COLS // parts, ROWS // strips
    frames = own * parts
    total_rows = frames * (width + 2)
    padded = -(-total_rows // LANES) * LANES
    bf16, f32 = jnp.bfloat16, jnp.float32
    operands = (offsets, spectra, column_planes(both // 2), row_planes(high), frame_weights(width, parts, padded))
    out = pl.pallas_call(
        functools.partial(kernel, parts, strips),
        out_shape=jax.ShapeDtypeStruct((width, frames, high), f32),
        in_specs=[pl.BlockSpec(memory_space=pltpu.SMEM)] + [pl.BlockSpec(memory_space=pl.ANY)] * 4,
        out_specs=pl.BlockSpec(memory_space=pltpu.VMEM),
        scratch_shapes=[pltpu.VMEM(operand.shape, operand.dtype) for operand in operands[1:]]
        + [
            pltpu.VMEM((COLS, 2 * depth), f32),
            pltpu.VMEM((COLS, 2 * depth), f32),
            pltpu.VMEM((parts, 8, 2 * depth), f32),
            pltpu.VMEM((parts, 2 * width, 2 * depth), bf16),
            pltpu.VMEM((parts, 8, 2 * depth), bf16),
            pltpu.VMEM((strips, parts, 2 * width, 2 * depth), bf16),
            pltpu.VMEM((strips, parts, 8, 2 * depth), bf16),
            pltpu.VMEM((total_rows, 2 * KR), bf16),
            pltpu.VMEM((total_rows, high), f32),
            pltpu.VMEM((padded, high), bf16),
            pltpu.SemaphoreType.DMA((4,)),
            pltpu.SemaphoreType.DMA((2,)),
            pltpu.SemaphoreType.DMA((2, parts)),
            pltpu.SemaphoreType.DMA((2, parts)),
            pltpu.SemaphoreType.DMA((2, parts)),
            pltpu.SemaphoreType.DMA((2, parts)),
        ],
        compiler_params=pltpu.CompilerParams(collective_id=0, has_side_effects=True, vmem_limit_bytes=48 << 20),
        name="sar",
    )(*operands)
    return jnp.transpose(out, (2, 0, 1))


def fits(mesh):
    parts, strips = mesh.shape["sub"], mesh.shape["strip"]
    return strips == 2 and KR // strips == LANES and COLS % parts == 0 and COLS // parts == 16 and parts % 4 == 0


def body(mesh, spectra, offsets):
    if fits(mesh) and spectra.shape[0] == 2:
        return kernel_body(spectra, offsets)
    return plain_body(spectra, offsets)


def solution(mesh):
    in_specs = (P("sub", "strip", None), P("sub"))
    out_specs = P("strip", "sub", None)
    return jax.shard_map(
        functools.partial(body, mesh), mesh=mesh, in_specs=in_specs, out_specs=out_specs, check_vma=False
    )
```

```python
import functools
import math

import jax
import jax.numpy as jnp
import numpy as np
from jax import lax
from jax.experimental import pallas as pl
from jax.experimental.pallas import tpu as pltpu
from jax.sharding import PartitionSpec as P

KR = 256
ROWS = 1024
COLS = 256
WIN = 8
BG = 16


def column_table(samples, parts):
    wide = COLS // parts + 2
    column = (np.arange(parts) * (wide - 2))[:, None] + np.arange(-1, wide - 1)[None, :]
    inside = (column >= 0) & (column < COLS)
    phase = ((np.arange(samples)[:, None, None] * column[None]) % samples) * (2.0 * math.pi / samples)
    cosine = np.where(inside, np.cos(phase), 0.0) / math.sqrt(samples)
    sine = np.where(inside, -np.sin(phase), 0.0) / math.sqrt(samples)
    upper = np.stack([cosine, sine], axis=2)
    lower = np.stack([-sine, cosine], axis=2)
    return jnp.asarray(np.concatenate([upper, lower], axis=0).astype(np.float32)).astype(jnp.bfloat16)


def row_table(rows):
    sample = jnp.arange(KR, dtype=jnp.int32)[:, None] - KR // 2
    phase = jnp.mod(rows[None, :] * sample, ROWS).astype(jnp.float32) * (2.0 * math.pi / ROWS)
    scale = jnp.where((rows >= 0) & (rows < ROWS), 1.0 / math.sqrt(KR), 0.0)[None, :]
    cosine = jnp.cos(phase) * scale
    sine = jnp.sin(phase) * scale
    upper = jnp.stack([cosine, sine], axis=1)
    lower = jnp.stack([-sine, cosine], axis=1)
    return jnp.concatenate([upper, lower], axis=0).astype(jnp.bfloat16)


def rotation(offsets, samples):
    angle = jnp.mod(offsets[:, None] * (samples[None, :] - KR // 2), ROWS).astype(jnp.float32) * (2.0 * math.pi / ROWS)
    return jnp.cos(angle), jnp.sin(angle)


def plain_body(spectra, offsets):
    own, depth = spectra.shape[:2]
    parts, strips = lax.axis_size("sub"), lax.axis_size("strip")
    wide = COLS // parts + 2
    high = ROWS // strips
    strip = lax.axis_index("strip")
    frames = own * parts
    table = column_table(spectra.shape[2] // 2, parts)
    cosine, sine = rotation(offsets, strip * depth + jnp.arange(depth, dtype=jnp.int32))
    mixed = jnp.einsum("skc,cdpn->dspnk", spectra, table, preferred_element_type=jnp.float32)
    real, imag = mixed[:, :, 0], mixed[:, :, 1]
    cosine, sine = cosine[None, :, None, :], sine[None, :, None, :]
    shifted = jnp.stack([real * cosine - imag * sine, real * sine + imag * cosine], axis=2).astype(jnp.bfloat16)
    held = lax.all_to_all(shifted, "sub", split_axis=0, concat_axis=0, tiled=True)
    held = held.reshape(frames, 2, wide, depth)
    whole = jnp.zeros((frames, 2, wide, strips, depth), jnp.bfloat16)
    for step in range(strips):
        part = held
        if step:
            part = lax.ppermute(held, "strip", [(i, (i + step) % strips) for i in range(strips)])
        source = jnp.mod(strip - step, strips)
        whole = lax.dynamic_update_slice(whole, part[:, :, :, None], (0, 0, 0, source, 0))
    wider = whole.reshape(frames, 2, wide, KR).astype(jnp.float32)
    summed = wider
    for lead in range(1, WIN):
        summed = summed + jnp.roll(wider, -lead, axis=0)
    rows = strip * high + jnp.arange(-1, high + 1, dtype=jnp.int32)
    product = jnp.einsum(
        "fpnk,pkqm->qnfm",
        summed.astype(jnp.bfloat16),
        row_table(rows).reshape(2, KR, 2, high + 2),
        preferred_element_type=jnp.float32,
    )
    log_power = jnp.log(1.0 + product[0] * product[0] + product[1] * product[1])
    total = log_power[:, :, :-2] + log_power[:, :, 1:-1] + log_power[:, :, 2:]
    filtered = (total[:-2] + total[1:-1] + total[2:]) / 9.0
    background = filtered
    for behind in range(1, BG):
        background = background + jnp.roll(filtered, behind, axis=1)
    return jnp.transpose(filtered - background / BG, (2, 0, 1))


LANES = 128
MESH = pl.DeviceIdType.MESH


def column_planes(samples):
    phase = (np.arange(COLS)[:, None] * np.arange(samples)[None, :] % samples) * (2.0 * math.pi / samples)
    planes = np.stack([np.cos(phase), -np.sin(phase)]) / math.sqrt(samples)
    return jnp.asarray(planes.astype(np.float32).astype(jnp.bfloat16))


def row_planes(high):
    row = np.concatenate([np.arange(high + LANES - 1), [-1]])
    used = (row <= high)[None, :]
    sample = np.arange(KR)[:, None] - KR // 2
    phase = (row[None, :] * sample % ROWS) * (2.0 * math.pi / ROWS)
    planes = np.stack([np.cos(phase) * used, np.sin(phase) * used]) / math.sqrt(KR)
    return jnp.asarray(planes.astype(np.float32).astype(jnp.bfloat16))


def frame_weights(width, sources, rows):
    frames = 2 * sources
    weights = np.zeros((width, frames, rows), np.float32)
    target = np.arange(frames)

    def place(at, column, frame):
        series = np.where(target == frame, 1.0, 0.0) - np.where((target - frame) % frames < BG, 1.0 / BG, 0.0)
        for near in range(max(column - 1, 0), min(column + 2, width)):
            weights[near, :, at] = series

    for lane in range(2):
        for source in range(sources):
            frame = 2 * source + lane
            for column in range(width):
                place((lane * sources + source) * width + column, column, frame)
            for side in range(2):
                place(2 * sources * width + (lane * sources + source) * 2 + side, (-1, width)[side], frame)
    return jnp.asarray(weights.reshape(width * frames, rows).astype(jnp.bfloat16))


def send_order(count):
    order = []
    for away in range(count // 2, 0, -1):
        order += [away] if 2 * away == count else [away, count - away]
    return order


def product_of(a, b):
    return lax.dot_general(a, b, (((1,), (0,)), ((), ())), preferred_element_type=jnp.float32)


def product_t(a, b):
    return lax.dot_general(a, b, (((1,), (1,)), ((), ())), preferred_element_type=jnp.float32)


def ahead(value, steps):
    return jnp.concatenate([value[steps:], value[:steps]], axis=0)


def kernel(
    parts, strips, offsets_hbm, spectra_hbm, columns_hbm, rows_hbm, weights_hbm, out_ref,
    offsets_ref, spectra, columns, rows, weights, real, imag, edge, main, halo, held, held_halo, lhs, boxed, level,
    load_sem, own_sem, send_sem, recv_sem, pass_sem, got_sem,
):
    me, strip = lax.axis_index("sub"), lax.axis_index("strip")
    width = COLS // parts
    depth = spectra.shape[1]
    samples = spectra.shape[2] // 2
    high = out_ref.shape[2]
    other = 1 - strip

    loads = [
        pltpu.make_async_copy(source, target, load_sem.at[i])
        for i, (source, target) in enumerate(
            [(offsets_hbm, offsets_ref), (spectra_hbm, spectra), (columns_hbm, columns), (rows_hbm, rows), (weights_hbm, weights)]
        )
    ]
    for load in loads:
        load.start()
    barrier = pltpu.get_barrier_semaphore()
    for away in range(1, parts):
        pl.semaphore_signal(barrier, inc=1, device_id=(lax.rem(me + away, parts), strip), device_id_type=MESH)
    pl.semaphore_signal(barrier, inc=1, device_id=(me, other), device_id_type=MESH)

    loads[0].wait()
    lane = lax.broadcasted_iota(jnp.int32, (1, 2 * depth), 1)
    sample = strip * depth + jnp.where(lane < depth, lane, lane - depth) - KR // 2
    offset = jnp.where(lane < depth, offsets_ref[0], offsets_ref[1])
    angle = jnp.bitwise_and(offset * sample, ROWS - 1).astype(jnp.float32) * (2.0 * math.pi / ROWS)
    cosine, sine = jnp.cos(angle), jnp.sin(angle)
    edge[...] = jnp.zeros_like(edge)
    loads[1].wait()
    loads[2].wait()
    data = spectra[...].reshape(2 * depth, 2 * samples)
    data_re, data_im = data[:, :samples], data[:, samples:]
    step = 64
    for at in range(0, COLS, step):
        cos_part, sin_part = columns[0, at : at + step], columns[1, at : at + step]
        re = product_t(cos_part, data_re) - product_t(sin_part, data_im)
        im = product_t(sin_part, data_re) + product_t(cos_part, data_im)
        first = at // width
        for part, value, ref in ((0, re * cosine - im * sine, real), (1, re * sine + im * cosine, imag)):
            ref[at : at + step] = value
            blocks = value.reshape(step // width, width, 2 * depth).astype(jnp.bfloat16)
            for own in range(2):
                main[first : first + step // width, own * width : (own + 1) * width, part * depth : (part + 1) * depth] = (
                    blocks[:, :, own * depth : (own + 1) * depth]
                )
    for part, ref in ((0, real), (1, imag)):
        for own in range(2):
            lanes, into = slice(own * depth, (own + 1) * depth), slice(part * depth, (part + 1) * depth)
            for d in range(parts):
                if d > 0:
                    edge[d, 2 * own : 2 * own + 1, into] = ref[d * width - 1 : d * width, lanes]
                if d < parts - 1:
                    edge[d, 2 * own + 1 : 2 * own + 2, into] = ref[(d + 1) * width : (d + 1) * width + 1, lanes]
    halo[...] = edge[...].astype(jnp.bfloat16)

    pl.semaphore_wait(barrier, parts)

    def sends(to, where):
        return [
            pltpu.make_async_remote_copy(
                src_ref=source.at[to], dst_ref=target.at[strip, where], send_sem=send_sem.at[kind, to],
                recv_sem=recv_sem.at[kind, where], device_id=(to, strip), device_id_type=MESH,
            )
            for kind, source, target in ((0, main, held), (1, halo, held_halo))
        ]

    def passes(h, source, own=False):
        return [
            pltpu.make_async_remote_copy(
                src_ref=block.at[source] if own else target.at[h, source], dst_ref=target.at[h, source],
                send_sem=pass_sem.at[kind, source], recv_sem=got_sem.at[kind, source],
                device_id=(me, other), device_id_type=MESH,
            )
            for kind, block, target in ((0, main, held), (1, halo, held_halo))
        ]

    order = send_order(parts)
    for away in order:
        for copy in sends(lax.rem(me + away, parts), me):
            copy.start()
    kept = [
        pltpu.make_async_copy(source.at[me], target.at[strip, me], own_sem.at[kind])
        for kind, source, target in ((0, main, held), (1, halo, held_halo))
    ]
    for copy in passes(strip, me, own=True) + kept:
        copy.start()
    for away in reversed(order):
        source = lax.rem(me + parts - away, parts)
        for copy in sends(source, source):
            copy.wait_recv()
        for copy in passes(strip, source):
            copy.start()
    for copy in kept:
        copy.wait()
    for away in [0] + order[::-1]:
        for copy in passes(other, lax.rem(me + parts - away, parts)):
            copy.wait_recv()
    for away in order:
        for copy in sends(lax.rem(me + away, parts), me):
            copy.wait_send()
    for away in [0] + order:
        for copy in passes(strip, lax.rem(me + away, parts), own=away == 0):
            copy.wait_send()

    top = 2 * parts * width
    odd = lax.rem(lax.broadcasted_iota(jnp.int32, (1, 1, 2 * depth), 2), 2)
    sign = 1.0 - 2.0 * (odd * strip).astype(jnp.float32)
    row_at = lax.broadcasted_iota(jnp.int32, (parts, 8, 2 * depth), 1)
    for h in range(2):
        block = held[h].astype(jnp.float32) * sign
        first, second = block[:, :width], block[:, width:]
        near = held_halo[h].astype(jnp.float32) * sign
        near_second = jnp.concatenate([pltpu.roll(near[i], 6, 0)[None] for i in range(parts)], axis=0)
        for is_halo, one, two in ((False, first, second), (True, near, near_second)):
            pair = one + two
            double = pair + ahead(pair, 1)
            quad = double + ahead(double, 2)
            for own, frame in ((0, quad), (1, quad - one + ahead(one, WIN // 2))):
                if is_halo:
                    frame = jnp.where(row_at < 2, frame, 0.0)
                    packed = []
                    for group in range(parts // 4):
                        total = frame[4 * group]
                        for j in range(1, 4):
                            total = total + pltpu.roll(frame[4 * group + j], 2 * j, 0)
                        packed.append(total)
                    flat = jnp.concatenate(packed, axis=0).astype(jnp.bfloat16)
                    at, size = top + own * 2 * parts, 2 * parts
                else:
                    flat = frame.reshape(parts * width, 2 * depth).astype(jnp.bfloat16)
                    at, size = own * parts * width, parts * width
                for part in range(2):
                    lhs[at : at + size, part * KR + h * depth : part * KR + (h + 1) * depth] = flat[
                        :, part * depth : (part + 1) * depth
                    ]

    loads[3].wait()
    total_rows = top + 4 * parts
    tail = lax.broadcasted_iota(jnp.int32, (1, high + LANES), 1)
    outside = ((tail == high) & (strip == strips - 1)) | ((tail == high + LANES - 1) & (strip == 0))
    inside = jnp.where(outside, 0.0, 1.0)
    chunk = 64
    for at in range(0, total_rows, chunk):
        left_re, left_im = lhs[at : at + chunk, :KR], lhs[at : at + chunk, KR:]
        re = product_of(left_re, rows[0]) - product_of(left_im, rows[1])
        im = product_of(left_re, rows[1]) + product_of(left_im, rows[0])
        power = jnp.log(1.0 + re * re + im * im) * inside
        summed = power + pltpu.roll(power, 1, 1) + pltpu.roll(power, high + LANES - 1, 1)
        boxed[at : at + chunk] = summed[:, :high]

    frames = 2 * parts
    block = boxed[:top].reshape(frames, width, high)
    mean = jnp.sum(block, axis=0, keepdims=True) * (1.0 / frames)
    level[:top] = (block - mean).reshape(top, high).astype(jnp.bfloat16)
    near = boxed[top:total_rows].reshape(frames // 4, 8, high)
    mean = jnp.sum(near, axis=0) * (1.0 / frames)
    mean = mean + pltpu.roll(mean, 4, 0)
    mean = mean + pltpu.roll(mean, 2, 0)
    level[top:total_rows] = (near - mean[None]).reshape(total_rows - top, high).astype(jnp.bfloat16)
    level[total_rows:] = jnp.zeros((level.shape[0] - total_rows, high), jnp.bfloat16)
    loads[4].wait()
    for c in range(0, width, 4):
        piece = product_of(weights[c * frames : (c + 4) * frames], level[...])
        out_ref[c : c + 4] = (piece * (1.0 / 9.0)).reshape(4, frames, high)


def kernel_body(spectra, offsets):
    parts, strips = lax.axis_size("sub"), lax.axis_size("strip")
    own, depth, both = spectra.shape
    width, high = COLS // parts, ROWS // strips
    frames = own * parts
    total_rows = frames * (width + 2)
    padded = -(-total_rows // LANES) * LANES
    bf16, f32 = jnp.bfloat16, jnp.float32
    operands = (offsets, spectra, column_planes(both // 2), row_planes(high), frame_weights(width, parts, padded))
    out = pl.pallas_call(
        functools.partial(kernel, parts, strips),
        out_shape=jax.ShapeDtypeStruct((width, frames, high), f32),
        in_specs=[pl.BlockSpec(memory_space=pltpu.HBM)] * 5,
        out_specs=pl.BlockSpec(memory_space=pltpu.VMEM),
        scratch_shapes=[pltpu.SMEM(offsets.shape, offsets.dtype)]
        + [pltpu.VMEM(operand.shape, operand.dtype) for operand in operands[1:]]
        + [
            pltpu.VMEM((COLS, 2 * depth), f32),
            pltpu.VMEM((COLS, 2 * depth), f32),
            pltpu.VMEM((parts, 8, 2 * depth), f32),
            pltpu.VMEM((parts, 2 * width, 2 * depth), bf16),
            pltpu.VMEM((parts, 8, 2 * depth), bf16),
            pltpu.VMEM((strips, parts, 2 * width, 2 * depth), bf16),
            pltpu.VMEM((strips, parts, 8, 2 * depth), bf16),
            pltpu.VMEM((total_rows, 2 * KR), bf16),
            pltpu.VMEM((total_rows, high), f32),
            pltpu.VMEM((padded, high), bf16),
            pltpu.SemaphoreType.DMA((5,)),
            pltpu.SemaphoreType.DMA((2,)),
            pltpu.SemaphoreType.DMA((2, parts)),
            pltpu.SemaphoreType.DMA((2, parts)),
            pltpu.SemaphoreType.DMA((2, parts)),
            pltpu.SemaphoreType.DMA((2, parts)),
        ],
        compiler_params=pltpu.CompilerParams(collective_id=0, has_side_effects=True, vmem_limit_bytes=48 << 20),
        name="sar",
    )(*(pltpu.with_memory_space_constraint(operand, pltpu.HBM) for operand in operands))
    return jnp.transpose(out, (2, 0, 1))


def fits(mesh):
    parts, strips = mesh.shape["sub"], mesh.shape["strip"]
    return strips == 2 and KR // strips == LANES and COLS % parts == 0 and COLS // parts == 16 and parts % 4 == 0


def body(mesh, spectra, offsets):
    if fits(mesh) and spectra.shape[0] == 2:
        return kernel_body(spectra, offsets)
    return plain_body(spectra, offsets)


def solution(mesh):
    in_specs = (P("sub", "strip", None), P("sub"))
    out_specs = P("strip", "sub", None)
    return jax.shard_map(
        functools.partial(body, mesh), mesh=mesh, in_specs=in_specs, out_specs=out_specs, check_vma=False
    )
```

```python
import functools
import math

import jax
import jax.numpy as jnp
import numpy as np
from jax import lax
from jax.experimental import pallas as pl
from jax.experimental.pallas import tpu as pltpu
from jax.sharding import PartitionSpec as P

KR = 256
ROWS = 1024
COLS = 256
WIN = 8
BG = 16


def column_table(samples, parts):
    wide = COLS // parts + 2
    column = (np.arange(parts) * (wide - 2))[:, None] + np.arange(-1, wide - 1)[None, :]
    inside = (column >= 0) & (column < COLS)
    phase = ((np.arange(samples)[:, None, None] * column[None]) % samples) * (2.0 * math.pi / samples)
    cosine = np.where(inside, np.cos(phase), 0.0) / math.sqrt(samples)
    sine = np.where(inside, -np.sin(phase), 0.0) / math.sqrt(samples)
    upper = np.stack([cosine, sine], axis=2)
    lower = np.stack([-sine, cosine], axis=2)
    return jnp.asarray(np.concatenate([upper, lower], axis=0).astype(np.float32)).astype(jnp.bfloat16)


def row_table(rows):
    sample = jnp.arange(KR, dtype=jnp.int32)[:, None] - KR // 2
    phase = jnp.mod(rows[None, :] * sample, ROWS).astype(jnp.float32) * (2.0 * math.pi / ROWS)
    scale = jnp.where((rows >= 0) & (rows < ROWS), 1.0 / math.sqrt(KR), 0.0)[None, :]
    cosine = jnp.cos(phase) * scale
    sine = jnp.sin(phase) * scale
    upper = jnp.stack([cosine, sine], axis=1)
    lower = jnp.stack([-sine, cosine], axis=1)
    return jnp.concatenate([upper, lower], axis=0).astype(jnp.bfloat16)


def rotation(offsets, samples):
    angle = jnp.mod(offsets[:, None] * (samples[None, :] - KR // 2), ROWS).astype(jnp.float32) * (2.0 * math.pi / ROWS)
    return jnp.cos(angle), jnp.sin(angle)


def plain_body(spectra, offsets):
    own, depth = spectra.shape[:2]
    parts, strips = lax.axis_size("sub"), lax.axis_size("strip")
    wide = COLS // parts + 2
    high = ROWS // strips
    strip = lax.axis_index("strip")
    frames = own * parts
    table = column_table(spectra.shape[2] // 2, parts)
    cosine, sine = rotation(offsets, strip * depth + jnp.arange(depth, dtype=jnp.int32))
    mixed = jnp.einsum("skc,cdpn->dspnk", spectra, table, preferred_element_type=jnp.float32)
    real, imag = mixed[:, :, 0], mixed[:, :, 1]
    cosine, sine = cosine[None, :, None, :], sine[None, :, None, :]
    shifted = jnp.stack([real * cosine - imag * sine, real * sine + imag * cosine], axis=2).astype(jnp.bfloat16)
    held = lax.all_to_all(shifted, "sub", split_axis=0, concat_axis=0, tiled=True)
    held = held.reshape(frames, 2, wide, depth)
    whole = jnp.zeros((frames, 2, wide, strips, depth), jnp.bfloat16)
    for step in range(strips):
        part = held
        if step:
            part = lax.ppermute(held, "strip", [(i, (i + step) % strips) for i in range(strips)])
        source = jnp.mod(strip - step, strips)
        whole = lax.dynamic_update_slice(whole, part[:, :, :, None], (0, 0, 0, source, 0))
    wider = whole.reshape(frames, 2, wide, KR).astype(jnp.float32)
    summed = wider
    for lead in range(1, WIN):
        summed = summed + jnp.roll(wider, -lead, axis=0)
    rows = strip * high + jnp.arange(-1, high + 1, dtype=jnp.int32)
    product = jnp.einsum(
        "fpnk,pkqm->qnfm",
        summed.astype(jnp.bfloat16),
        row_table(rows).reshape(2, KR, 2, high + 2),
        preferred_element_type=jnp.float32,
    )
    log_power = jnp.log(1.0 + product[0] * product[0] + product[1] * product[1])
    total = log_power[:, :, :-2] + log_power[:, :, 1:-1] + log_power[:, :, 2:]
    filtered = (total[:-2] + total[1:-1] + total[2:]) / 9.0
    background = filtered
    for behind in range(1, BG):
        background = background + jnp.roll(filtered, behind, axis=1)
    return jnp.transpose(filtered - background / BG, (2, 0, 1))


LANES = 128
MESH = pl.DeviceIdType.MESH


def column_planes(samples):
    phase = (np.arange(COLS)[:, None] * np.arange(samples)[None, :] % samples) * (2.0 * math.pi / samples)
    planes = np.stack([np.cos(phase), -np.sin(phase)]) / math.sqrt(samples)
    return jnp.asarray(planes.astype(np.float32).astype(jnp.bfloat16))


def row_planes(high):
    row = np.concatenate([np.arange(high + LANES - 1), [-1]])
    used = (row <= high)[None, :]
    sample = np.arange(KR)[:, None] - KR // 2
    phase = (row[None, :] * sample % ROWS) * (2.0 * math.pi / ROWS)
    planes = np.stack([np.cos(phase) * used, np.sin(phase) * used]) / math.sqrt(KR)
    return jnp.asarray(planes.astype(np.float32).astype(jnp.bfloat16))


def frame_weights(width, sources, rows):
    frames = 2 * sources
    weights = np.zeros((width, frames, rows), np.float32)
    target = np.arange(frames)

    def place(at, column, frame):
        series = np.where(target == frame, 1.0, 0.0) - np.where((target - frame) % frames < BG, 1.0 / BG, 0.0)
        for near in range(max(column - 1, 0), min(column + 2, width)):
            weights[near, :, at] = series

    for lane in range(2):
        for source in range(sources):
            frame = 2 * source + lane
            for column in range(width):
                place((lane * sources + source) * width + column, column, frame)
            for side in range(2):
                place(2 * sources * width + (lane * sources + source) * 2 + side, (-1, width)[side], frame)
    return jnp.asarray(weights.reshape(width * frames, rows).astype(jnp.bfloat16))


def send_order(count):
    order = []
    for away in range(count // 2, 0, -1):
        order += [away] if 2 * away == count else [away, count - away]
    return order


def product_of(a, b):
    return lax.dot_general(a, b, (((1,), (0,)), ((), ())), preferred_element_type=jnp.float32)


def product_t(a, b):
    return lax.dot_general(a, b, (((1,), (1,)), ((), ())), preferred_element_type=jnp.float32)


def ahead(value, steps):
    return jnp.concatenate([value[steps:], value[:steps]], axis=0)


def kernel(
    parts, strips, offsets_hbm, spectra_hbm, columns_hbm, rows_hbm, weights_hbm, out_ref,
    offsets_ref, spectra, columns, rows, weights, real, imag, edge, main, halo, held, held_halo, lhs, boxed, level,
    load_sem, own_sem, send_sem, recv_sem, pass_sem, got_sem,
):
    me, strip = lax.axis_index("sub"), lax.axis_index("strip")
    width = COLS // parts
    depth = spectra.shape[1]
    samples = spectra.shape[2] // 2
    high = out_ref.shape[2]
    other = 1 - strip

    loads = [
        pltpu.make_async_copy(source, target, load_sem.at[i])
        for i, (source, target) in enumerate(
            [(offsets_hbm, offsets_ref), (spectra_hbm, spectra), (columns_hbm, columns), (rows_hbm, rows), (weights_hbm, weights)]
        )
    ]
    for load in loads[:3]:
        load.start()
    barrier = pltpu.get_barrier_semaphore()
    for away in range(1, parts):
        pl.semaphore_signal(barrier, inc=1, device_id=(lax.rem(me + away, parts), strip), device_id_type=MESH)
    pl.semaphore_signal(barrier, inc=1, device_id=(me, other), device_id_type=MESH)

    loads[0].wait()
    lane = lax.broadcasted_iota(jnp.int32, (1, 2 * depth), 1)
    sample = strip * depth + jnp.where(lane < depth, lane, lane - depth) - KR // 2
    offset = jnp.where(lane < depth, offsets_ref[0], offsets_ref[1])
    angle = jnp.bitwise_and(offset * sample, ROWS - 1).astype(jnp.float32) * (2.0 * math.pi / ROWS)
    cosine, sine = jnp.cos(angle), jnp.sin(angle)
    edge[...] = jnp.zeros_like(edge)
    loads[1].wait()
    loads[2].wait()
    for load in loads[3:]:
        load.start()
    data = spectra[...].reshape(2 * depth, 2 * samples)
    data_re, data_im = data[:, :samples], data[:, samples:]
    step = COLS
    for at in range(0, COLS, step):
        cos_part, sin_part = columns[0, at : at + step], columns[1, at : at + step]
        re = product_t(cos_part, data_re) - product_t(sin_part, data_im)
        im = product_t(sin_part, data_re) + product_t(cos_part, data_im)
        first = at // width
        for part, value, ref in ((0, re * cosine - im * sine, real), (1, re * sine + im * cosine, imag)):
            ref[at : at + step] = value
            blocks = value.reshape(step // width, width, 2 * depth).astype(jnp.bfloat16)
            for own in range(2):
                main[first : first + step // width, own * width : (own + 1) * width, part * depth : (part + 1) * depth] = (
                    blocks[:, :, own * depth : (own + 1) * depth]
                )
    for part, ref in ((0, real), (1, imag)):
        for own in range(2):
            lanes, into = slice(own * depth, (own + 1) * depth), slice(part * depth, (part + 1) * depth)
            for d in range(parts):
                if d > 0:
                    edge[d, 2 * own : 2 * own + 1, into] = ref[d * width - 1 : d * width, lanes]
                if d < parts - 1:
                    edge[d, 2 * own + 1 : 2 * own + 2, into] = ref[(d + 1) * width : (d + 1) * width + 1, lanes]
    halo[...] = edge[...].astype(jnp.bfloat16)

    pl.semaphore_wait(barrier, parts)

    def sends(to, where):
        return [
            pltpu.make_async_remote_copy(
                src_ref=source.at[to], dst_ref=target.at[strip, where], send_sem=send_sem.at[kind, to],
                recv_sem=recv_sem.at[kind, where], device_id=(to, strip), device_id_type=MESH,
            )
            for kind, source, target in ((0, main, held), (1, halo, held_halo))
        ]

    def passes(h, source, own=False):
        return [
            pltpu.make_async_remote_copy(
                src_ref=block.at[source] if own else target.at[h, source], dst_ref=target.at[h, source],
                send_sem=pass_sem.at[kind, source], recv_sem=got_sem.at[kind, source],
                device_id=(me, other), device_id_type=MESH,
            )
            for kind, block, target in ((0, main, held), (1, halo, held_halo))
        ]

    order = send_order(parts)
    for away in order:
        for copy in sends(lax.rem(me + away, parts), me):
            copy.start()
    kept = [
        pltpu.make_async_copy(source.at[me], target.at[strip, me], own_sem.at[kind])
        for kind, source, target in ((0, main, held), (1, halo, held_halo))
    ]
    for copy in passes(strip, me, own=True) + kept:
        copy.start()
    for away in reversed(order):
        source = lax.rem(me + parts - away, parts)
        for copy in sends(source, source):
            copy.wait_recv()
        for copy in passes(strip, source):
            copy.start()
    top = 2 * parts * width
    odd = lax.rem(lax.broadcasted_iota(jnp.int32, (1, 1, 2 * depth), 2), 2)
    sign = 1.0 - 2.0 * (odd * strip).astype(jnp.float32)
    row_at = lax.broadcasted_iota(jnp.int32, (parts, 8, 2 * depth), 1)
    def window(h):
        block = held[h].astype(jnp.float32) * sign
        first, second = block[:, :width], block[:, width:]
        near = held_halo[h].astype(jnp.float32) * sign
        near_second = jnp.concatenate([pltpu.roll(near[i], 6, 0)[None] for i in range(parts)], axis=0)
        for is_halo, one, two in ((False, first, second), (True, near, near_second)):
            pair = one + two
            double = pair + ahead(pair, 1)
            quad = double + ahead(double, 2)
            for own, frame in ((0, quad), (1, quad - one + ahead(one, WIN // 2))):
                if is_halo:
                    frame = jnp.where(row_at < 2, frame, 0.0)
                    packed = []
                    for group in range(parts // 4):
                        total = frame[4 * group]
                        for j in range(1, 4):
                            total = total + pltpu.roll(frame[4 * group + j], 2 * j, 0)
                        packed.append(total)
                    flat = jnp.concatenate(packed, axis=0).astype(jnp.bfloat16)
                    at, size = top + own * 2 * parts, 2 * parts
                else:
                    flat = frame.reshape(parts * width, 2 * depth).astype(jnp.bfloat16)
                    at, size = own * parts * width, parts * width
                for part in range(2):
                    lhs[at : at + size, pl.ds(pl.multiple_of(part * KR + h * depth, depth), depth)] = flat[
                        :, part * depth : (part + 1) * depth
                    ]

    for copy in kept:
        copy.wait()
    window(strip)
    for away in [0] + order[::-1]:
        for copy in passes(other, lax.rem(me + parts - away, parts)):
            copy.wait_recv()
    window(other)
    loads[3].wait()
    total_rows = top + 4 * parts
    tail = lax.broadcasted_iota(jnp.int32, (1, high + LANES), 1)
    outside = ((tail == high) & (strip == strips - 1)) | ((tail == high + LANES - 1) & (strip == 0))
    inside = jnp.where(outside, 0.0, 1.0)
    chunk = total_rows // 3
    for at in range(0, total_rows, chunk):
        left_re, left_im = lhs[at : at + chunk, :KR], lhs[at : at + chunk, KR:]
        re = product_of(left_re, rows[0]) - product_of(left_im, rows[1])
        im = product_of(left_re, rows[1]) + product_of(left_im, rows[0])
        power = jnp.log(1.0 + re * re + im * im) * inside
        summed = power + pltpu.roll(power, 1, 1) + pltpu.roll(power, high + LANES - 1, 1)
        boxed[at : at + chunk] = summed[:, :high]

    frames = 2 * parts
    block = boxed[:top].reshape(frames, width, high)
    mean = jnp.sum(block, axis=0, keepdims=True) * (1.0 / frames)
    level[:top] = (block - mean).reshape(top, high).astype(jnp.bfloat16)
    near = boxed[top:total_rows].reshape(frames // 4, 8, high)
    mean = jnp.sum(near, axis=0) * (1.0 / frames)
    mean = mean + pltpu.roll(mean, 4, 0)
    mean = mean + pltpu.roll(mean, 2, 0)
    level[top:total_rows] = (near - mean[None]).reshape(total_rows - top, high).astype(jnp.bfloat16)
    level[total_rows:] = jnp.zeros((level.shape[0] - total_rows, high), jnp.bfloat16)
    loads[4].wait()
    for c in range(0, width, 4):
        piece = product_of(weights[c * frames : (c + 4) * frames], level[...])
        out_ref[c : c + 4] = (piece * (1.0 / 9.0)).reshape(4, frames, high)
    for away in order:
        for copy in sends(lax.rem(me + away, parts), me):
            copy.wait_send()
    for away in [0] + order:
        for copy in passes(strip, lax.rem(me + away, parts), own=away == 0):
            copy.wait_send()


def kernel_body(spectra, offsets):
    parts, strips = lax.axis_size("sub"), lax.axis_size("strip")
    own, depth, both = spectra.shape
    width, high = COLS // parts, ROWS // strips
    frames = own * parts
    total_rows = frames * (width + 2)
    padded = -(-total_rows // LANES) * LANES
    bf16, f32 = jnp.bfloat16, jnp.float32
    operands = (offsets, spectra, column_planes(both // 2), row_planes(high), frame_weights(width, parts, padded))
    out = pl.pallas_call(
        functools.partial(kernel, parts, strips),
        out_shape=jax.ShapeDtypeStruct((width, frames, high), f32),
        in_specs=[pl.BlockSpec(memory_space=pltpu.HBM)] * 5,
        out_specs=pl.BlockSpec(memory_space=pltpu.VMEM),
        scratch_shapes=[pltpu.SMEM(offsets.shape, offsets.dtype)]
        + [pltpu.VMEM(operand.shape, operand.dtype) for operand in operands[1:]]
        + [
            pltpu.VMEM((COLS, 2 * depth), f32),
            pltpu.VMEM((COLS, 2 * depth), f32),
            pltpu.VMEM((parts, 8, 2 * depth), f32),
            pltpu.VMEM((parts, 2 * width, 2 * depth), bf16),
            pltpu.VMEM((parts, 8, 2 * depth), bf16),
            pltpu.VMEM((strips, parts, 2 * width, 2 * depth), bf16),
            pltpu.VMEM((strips, parts, 8, 2 * depth), bf16),
            pltpu.VMEM((total_rows, 2 * KR), bf16),
            pltpu.VMEM((total_rows, high), f32),
            pltpu.VMEM((padded, high), bf16),
            pltpu.SemaphoreType.DMA((5,)),
            pltpu.SemaphoreType.DMA((2,)),
            pltpu.SemaphoreType.DMA((2, parts)),
            pltpu.SemaphoreType.DMA((2, parts)),
            pltpu.SemaphoreType.DMA((2, parts)),
            pltpu.SemaphoreType.DMA((2, parts)),
        ],
        compiler_params=pltpu.CompilerParams(collective_id=0, has_side_effects=True, vmem_limit_bytes=48 << 20),
        name="sar",
    )(*(pltpu.with_memory_space_constraint(operand, pltpu.HBM) for operand in operands))
    return jnp.transpose(out, (2, 0, 1))


def fits(mesh):
    parts, strips = mesh.shape["sub"], mesh.shape["strip"]
    return strips == 2 and KR // strips == LANES and COLS % parts == 0 and COLS // parts == 16 and parts % 4 == 0


def body(mesh, spectra, offsets):
    if fits(mesh) and spectra.shape[0] == 2:
        return kernel_body(spectra, offsets)
    return plain_body(spectra, offsets)


def solution(mesh):
    in_specs = (P("sub", "strip", None), P("sub"))
    out_specs = P("strip", "sub", None)
    return jax.shard_map(
        functools.partial(body, mesh), mesh=mesh, in_specs=in_specs, out_specs=out_specs, check_vma=False
    )
```

```python
import functools
import math

import jax
import jax.numpy as jnp
import numpy as np
from jax import lax
from jax.experimental import pallas as pl
from jax.experimental.pallas import tpu as pltpu
from jax.sharding import PartitionSpec as P

KR = 256
ROWS = 1024
COLS = 256
WIN = 8
BG = 16


def column_table(samples, parts):
    wide = COLS // parts + 2
    column = (np.arange(parts) * (wide - 2))[:, None] + np.arange(-1, wide - 1)[None, :]
    inside = (column >= 0) & (column < COLS)
    phase = ((np.arange(samples)[:, None, None] * column[None]) % samples) * (2.0 * math.pi / samples)
    cosine = np.where(inside, np.cos(phase), 0.0) / math.sqrt(samples)
    sine = np.where(inside, -np.sin(phase), 0.0) / math.sqrt(samples)
    upper = np.stack([cosine, sine], axis=2)
    lower = np.stack([-sine, cosine], axis=2)
    return jnp.asarray(np.concatenate([upper, lower], axis=0).astype(np.float32)).astype(jnp.bfloat16)


def row_table(rows):
    sample = jnp.arange(KR, dtype=jnp.int32)[:, None] - KR // 2
    phase = jnp.mod(rows[None, :] * sample, ROWS).astype(jnp.float32) * (2.0 * math.pi / ROWS)
    scale = jnp.where((rows >= 0) & (rows < ROWS), 1.0 / math.sqrt(KR), 0.0)[None, :]
    cosine = jnp.cos(phase) * scale
    sine = jnp.sin(phase) * scale
    upper = jnp.stack([cosine, sine], axis=1)
    lower = jnp.stack([-sine, cosine], axis=1)
    return jnp.concatenate([upper, lower], axis=0).astype(jnp.bfloat16)


def rotation(offsets, samples):
    angle = jnp.mod(offsets[:, None] * (samples[None, :] - KR // 2), ROWS).astype(jnp.float32) * (2.0 * math.pi / ROWS)
    return jnp.cos(angle), jnp.sin(angle)


def plain_body(spectra, offsets):
    own, depth = spectra.shape[:2]
    parts, strips = lax.axis_size("sub"), lax.axis_size("strip")
    wide = COLS // parts + 2
    high = ROWS // strips
    strip = lax.axis_index("strip")
    frames = own * parts
    table = column_table(spectra.shape[2] // 2, parts)
    cosine, sine = rotation(offsets, strip * depth + jnp.arange(depth, dtype=jnp.int32))
    mixed = jnp.einsum("skc,cdpn->dspnk", spectra, table, preferred_element_type=jnp.float32)
    real, imag = mixed[:, :, 0], mixed[:, :, 1]
    cosine, sine = cosine[None, :, None, :], sine[None, :, None, :]
    shifted = jnp.stack([real * cosine - imag * sine, real * sine + imag * cosine], axis=2).astype(jnp.bfloat16)
    held = lax.all_to_all(shifted, "sub", split_axis=0, concat_axis=0, tiled=True)
    held = held.reshape(frames, 2, wide, depth)
    whole = jnp.zeros((frames, 2, wide, strips, depth), jnp.bfloat16)
    for step in range(strips):
        part = held
        if step:
            part = lax.ppermute(held, "strip", [(i, (i + step) % strips) for i in range(strips)])
        source = jnp.mod(strip - step, strips)
        whole = lax.dynamic_update_slice(whole, part[:, :, :, None], (0, 0, 0, source, 0))
    wider = whole.reshape(frames, 2, wide, KR).astype(jnp.float32)
    summed = wider
    for lead in range(1, WIN):
        summed = summed + jnp.roll(wider, -lead, axis=0)
    rows = strip * high + jnp.arange(-1, high + 1, dtype=jnp.int32)
    product = jnp.einsum(
        "fpnk,pkqm->qnfm",
        summed.astype(jnp.bfloat16),
        row_table(rows).reshape(2, KR, 2, high + 2),
        preferred_element_type=jnp.float32,
    )
    log_power = jnp.log(1.0 + product[0] * product[0] + product[1] * product[1])
    total = log_power[:, :, :-2] + log_power[:, :, 1:-1] + log_power[:, :, 2:]
    filtered = (total[:-2] + total[1:-1] + total[2:]) / 9.0
    background = filtered
    for behind in range(1, BG):
        background = background + jnp.roll(filtered, behind, axis=1)
    return jnp.transpose(filtered - background / BG, (2, 0, 1))


LANES = 128
GROUP = 4
MESH = pl.DeviceIdType.MESH


def column_planes(samples):
    phase = (np.arange(COLS)[:, None] * np.arange(samples)[None, :] % samples) * (2.0 * math.pi / samples)
    planes = np.stack([np.cos(phase), -np.sin(phase)]) / math.sqrt(samples)
    return jnp.asarray(planes.astype(np.float32).astype(jnp.bfloat16))


def row_planes(high):
    row = np.concatenate([np.arange(high + LANES - 1), [-1]])
    used = (row <= high)[None, :]
    sample = np.arange(KR)[:, None] - KR // 2
    phase = (row[None, :] * sample % ROWS) * (2.0 * math.pi / ROWS)
    planes = np.stack([np.cos(phase) * used, np.sin(phase) * used]) / math.sqrt(KR)
    return jnp.asarray(planes.astype(np.float32).astype(jnp.bfloat16))


def frame_weights(width, sources, rows):
    frames = 2 * sources
    weights = np.zeros((width, frames, rows), np.float32)
    target = np.arange(frames)

    def place(at, column, frame):
        series = np.where(target == frame, 1.0, 0.0) - np.where((target - frame) % frames < BG, 1.0 / BG, 0.0)
        for near in range(max(column - 1, 0), min(column + 2, width)):
            weights[near, :, at] = series

    for lane in range(2):
        for source in range(sources):
            frame = 2 * source + lane
            for column in range(width):
                place((lane * sources + source) * width + column, column, frame)
            for side in range(2):
                place(2 * sources * width + (lane * sources + source) * 2 + side, (-1, width)[side], frame)
    return jnp.asarray(weights.reshape(width * frames, rows).astype(jnp.bfloat16))


def send_order(layers, group):
    order = [(0, place) for place in range(1, group)]
    half = layers // 2
    turn = [half] + [layer for away in range(half - 1, 0, -1) for layer in (half - away, half + away)]
    return order + [(layer, place) for place in range(group) for layer in turn]


def product_of(a, b):
    return lax.dot_general(a, b, (((1,), (0,)), ((), ())), preferred_element_type=jnp.float32)


def product_t(a, b):
    return lax.dot_general(a, b, (((1,), (1,)), ((), ())), preferred_element_type=jnp.float32)


def ahead(value, steps):
    return jnp.concatenate([value[steps:], value[:steps]], axis=0)


def kernel(
    parts, strips, offsets_hbm, spectra_hbm, columns_hbm, rows_hbm, weights_hbm, out_ref,
    offsets_ref, spectra, columns, rows, weights, real, imag, edge, main, halo, held, held_halo, lhs, boxed, level,
    load_sem, own_sem, send_sem, recv_sem, pass_sem, got_sem,
):
    me, strip = lax.axis_index("sub"), lax.axis_index("strip")
    width = COLS // parts
    depth = spectra.shape[1]
    samples = spectra.shape[2] // 2
    high = out_ref.shape[2]
    other = 1 - strip

    loads = [
        pltpu.make_async_copy(source, target, load_sem.at[i])
        for i, (source, target) in enumerate(
            [(offsets_hbm, offsets_ref), (spectra_hbm, spectra), (columns_hbm, columns), (rows_hbm, rows), (weights_hbm, weights)]
        )
    ]
    for load in loads[:3]:
        load.start()
    barrier = pltpu.get_barrier_semaphore()
    for away in range(1, parts):
        pl.semaphore_signal(barrier, inc=1, device_id=(lax.rem(me + away, parts), strip), device_id_type=MESH)
    pl.semaphore_signal(barrier, inc=1, device_id=(me, other), device_id_type=MESH)

    loads[0].wait()
    lane = lax.broadcasted_iota(jnp.int32, (1, 2 * depth), 1)
    sample = strip * depth + jnp.where(lane < depth, lane, lane - depth) - KR // 2
    offset = jnp.where(lane < depth, offsets_ref[0], offsets_ref[1])
    angle = jnp.bitwise_and(offset * sample, ROWS - 1).astype(jnp.float32) * (2.0 * math.pi / ROWS)
    cosine, sine = jnp.cos(angle), jnp.sin(angle)
    edge[...] = jnp.zeros_like(edge)
    loads[1].wait()
    loads[2].wait()
    for load in loads[3:]:
        load.start()
    data = spectra[...].reshape(2 * depth, 2 * samples)
    data_re, data_im = data[:, :samples], data[:, samples:]
    step = COLS
    for at in range(0, COLS, step):
        cos_part, sin_part = columns[0, at : at + step], columns[1, at : at + step]
        re = product_t(cos_part, data_re) - product_t(sin_part, data_im)
        im = product_t(sin_part, data_re) + product_t(cos_part, data_im)
        first = at // width
        for part, value, ref in ((0, re * cosine - im * sine, real), (1, re * sine + im * cosine, imag)):
            ref[at : at + step] = value
            blocks = value.reshape(step // width, width, 2 * depth).astype(jnp.bfloat16)
            for own in range(2):
                main[first : first + step // width, own * width : (own + 1) * width, part * depth : (part + 1) * depth] = (
                    blocks[:, :, own * depth : (own + 1) * depth]
                )
    for part, ref in ((0, real), (1, imag)):
        for own in range(2):
            lanes, into = slice(own * depth, (own + 1) * depth), slice(part * depth, (part + 1) * depth)
            for d in range(parts):
                if d > 0:
                    edge[d, 2 * own : 2 * own + 1, into] = ref[d * width - 1 : d * width, lanes]
                if d < parts - 1:
                    edge[d, 2 * own + 1 : 2 * own + 2, into] = ref[(d + 1) * width : (d + 1) * width + 1, lanes]
    halo[...] = edge[:, :4].astype(jnp.bfloat16)

    pl.semaphore_wait(barrier, parts)

    def sends(to, where):
        return [
            pltpu.make_async_remote_copy(
                src_ref=source.at[to], dst_ref=target.at[strip, where], send_sem=send_sem.at[kind, to],
                recv_sem=recv_sem.at[kind, where], device_id=(to, strip), device_id_type=MESH,
            )
            for kind, source, target in ((0, main, held), (1, halo, held_halo))
        ]

    def passes(h, source, own=False):
        return [
            pltpu.make_async_remote_copy(
                src_ref=block.at[source] if own else target.at[h, source], dst_ref=target.at[h, source],
                send_sem=pass_sem.at[kind, source], recv_sem=got_sem.at[kind, source],
                device_id=(me, other), device_id_type=MESH,
            )
            for kind, block, target in ((0, main, held), (1, halo, held_halo))
        ]

    layers = parts // GROUP
    order = send_order(layers, GROUP)

    def device_at(layer, place):
        return lax.rem(me // GROUP + layer, layers) * GROUP + lax.rem(lax.rem(me, GROUP) + place, GROUP)

    def device_from(layer, place):
        return device_at(layers - layer, GROUP - place)

    for away in order:
        for copy in sends(device_at(*away), me):
            copy.start()
    kept = [
        pltpu.make_async_copy(source.at[me], target.at[strip, me], own_sem.at[kind])
        for kind, source, target in ((0, main, held), (1, halo, held_halo))
    ]
    for copy in passes(strip, me, own=True) + kept:
        copy.start()
    for away in order:
        source = device_from(*away)
        for copy in sends(source, source):
            copy.wait_recv()
        for copy in passes(strip, source):
            copy.start()
    top = 2 * parts * width
    odd = lax.rem(lax.broadcasted_iota(jnp.int32, (1, 1, 2 * depth), 2), 2)
    sign = 1.0 - 2.0 * (odd * strip).astype(jnp.float32)
    row_at = lax.broadcasted_iota(jnp.int32, (parts, 8, 2 * depth), 1)
    def window(h):
        block = held[h].astype(jnp.float32) * sign
        first, second = block[:, :width], block[:, width:]
        near = held_halo[h].astype(jnp.float32) * sign
        near = jnp.concatenate([near, jnp.zeros_like(near)], axis=1)
        near_second = jnp.concatenate([pltpu.roll(near[i], 6, 0)[None] for i in range(parts)], axis=0)
        for is_halo, one, two in ((False, first, second), (True, near, near_second)):
            pair = one + two
            double = pair + ahead(pair, 1)
            quad = double + ahead(double, 2)
            for own, frame in ((0, quad), (1, quad - one + ahead(one, WIN // 2))):
                if is_halo:
                    frame = jnp.where(row_at < 2, frame, 0.0)
                    packed = []
                    for group in range(parts // 4):
                        total = frame[4 * group]
                        for j in range(1, 4):
                            total = total + pltpu.roll(frame[4 * group + j], 2 * j, 0)
                        packed.append(total)
                    flat = jnp.concatenate(packed, axis=0).astype(jnp.bfloat16)
                    at, size = top + own * 2 * parts, 2 * parts
                else:
                    flat = frame.reshape(parts * width, 2 * depth).astype(jnp.bfloat16)
                    at, size = own * parts * width, parts * width
                for part in range(2):
                    lhs[at : at + size, pl.ds(pl.multiple_of(part * KR + h * depth, depth), depth)] = flat[
                        :, part * depth : (part + 1) * depth
                    ]

    for copy in kept:
        copy.wait()
    window(strip)
    for away in [(0, 0)] + order:
        for copy in passes(other, device_from(*away)):
            copy.wait_recv()
    window(other)
    loads[3].wait()
    total_rows = top + 4 * parts
    tail = lax.broadcasted_iota(jnp.int32, (1, high + LANES), 1)
    outside = ((tail == high) & (strip == strips - 1)) | ((tail == high + LANES - 1) & (strip == 0))
    inside = jnp.where(outside, 0.0, 1.0)
    chunk = total_rows // 3
    for at in range(0, total_rows, chunk):
        left_re, left_im = lhs[at : at + chunk, :KR], lhs[at : at + chunk, KR:]
        re = product_of(left_re, rows[0]) - product_of(left_im, rows[1])
        im = product_of(left_re, rows[1]) + product_of(left_im, rows[0])
        power = jnp.log(1.0 + re * re + im * im) * inside
        summed = power + pltpu.roll(power, 1, 1) + pltpu.roll(power, high + LANES - 1, 1)
        boxed[at : at + chunk] = summed[:, :high]

    frames = 2 * parts
    block = boxed[:top].reshape(frames, width, high)
    mean = jnp.sum(block, axis=0, keepdims=True) * (1.0 / frames)
    level[:top] = (block - mean).reshape(top, high).astype(jnp.bfloat16)
    near = boxed[top:total_rows].reshape(frames // 4, 8, high)
    mean = jnp.sum(near, axis=0) * (1.0 / frames)
    mean = mean + pltpu.roll(mean, 4, 0)
    mean = mean + pltpu.roll(mean, 2, 0)
    level[top:total_rows] = (near - mean[None]).reshape(total_rows - top, high).astype(jnp.bfloat16)
    level[total_rows:] = jnp.zeros((level.shape[0] - total_rows, high), jnp.bfloat16)
    loads[4].wait()
    for c in range(0, width, 4):
        piece = product_of(weights[c * frames : (c + 4) * frames], level[...])
        out_ref[c : c + 4] = (piece * (1.0 / 9.0)).reshape(4, frames, high)
    for away in order:
        for copy in sends(device_at(*away), me):
            copy.wait_send()
    for away in [(0, 0)] + order:
        for copy in passes(strip, device_from(*away), own=away == (0, 0)):
            copy.wait_send()


def kernel_body(spectra, offsets):
    parts, strips = lax.axis_size("sub"), lax.axis_size("strip")
    own, depth, both = spectra.shape
    width, high = COLS // parts, ROWS // strips
    frames = own * parts
    total_rows = frames * (width + 2)
    padded = -(-total_rows // LANES) * LANES
    bf16, f32 = jnp.bfloat16, jnp.float32
    operands = (offsets, spectra, column_planes(both // 2), row_planes(high), frame_weights(width, parts, padded))
    out = pl.pallas_call(
        functools.partial(kernel, parts, strips),
        out_shape=jax.ShapeDtypeStruct((width, frames, high), f32),
        in_specs=[pl.BlockSpec(memory_space=pltpu.HBM)] * 5,
        out_specs=pl.BlockSpec(memory_space=pltpu.VMEM),
        scratch_shapes=[pltpu.SMEM(offsets.shape, offsets.dtype)]
        + [pltpu.VMEM(operand.shape, operand.dtype) for operand in operands[1:]]
        + [
            pltpu.VMEM((COLS, 2 * depth), f32),
            pltpu.VMEM((COLS, 2 * depth), f32),
            pltpu.VMEM((parts, 8, 2 * depth), f32),
            pltpu.VMEM((parts, 2 * width, 2 * depth), bf16),
            pltpu.VMEM((parts, 4, 2 * depth), bf16),
            pltpu.VMEM((strips, parts, 2 * width, 2 * depth), bf16),
            pltpu.VMEM((strips, parts, 4, 2 * depth), bf16),
            pltpu.VMEM((total_rows, 2 * KR), bf16),
            pltpu.VMEM((total_rows, high), f32),
            pltpu.VMEM((padded, high), bf16),
            pltpu.SemaphoreType.DMA((5,)),
            pltpu.SemaphoreType.DMA((2,)),
            pltpu.SemaphoreType.DMA((2, parts)),
            pltpu.SemaphoreType.DMA((2, parts)),
            pltpu.SemaphoreType.DMA((2, parts)),
            pltpu.SemaphoreType.DMA((2, parts)),
        ],
        compiler_params=pltpu.CompilerParams(collective_id=0, has_side_effects=True, vmem_limit_bytes=48 << 20),
        name="sar",
    )(*(pltpu.with_memory_space_constraint(operand, pltpu.HBM) for operand in operands))
    return jnp.transpose(out, (2, 0, 1))


def fits(mesh):
    parts, strips = mesh.shape["sub"], mesh.shape["strip"]
    return strips == 2 and KR // strips == LANES and COLS % parts == 0 and COLS // parts == 16 and parts % 4 == 0


def body(mesh, spectra, offsets):
    if fits(mesh) and spectra.shape[0] == 2:
        return kernel_body(spectra, offsets)
    return plain_body(spectra, offsets)


def solution(mesh):
    in_specs = (P("sub", "strip", None), P("sub"))
    out_specs = P("strip", "sub", None)
    return jax.shard_map(
        functools.partial(body, mesh), mesh=mesh, in_specs=in_specs, out_specs=out_specs, check_vma=False
    )
```

```python
import functools
import math

import jax
import jax.numpy as jnp
import numpy as np
from jax import lax
from jax.experimental import pallas as pl
from jax.experimental.pallas import tpu as pltpu
from jax.sharding import PartitionSpec as P

KR = 256
ROWS = 1024
COLS = 256
WIN = 8
BG = 16


def column_table(samples, parts):
    wide = COLS // parts + 2
    column = (np.arange(parts) * (wide - 2))[:, None] + np.arange(-1, wide - 1)[None, :]
    inside = (column >= 0) & (column < COLS)
    phase = ((np.arange(samples)[:, None, None] * column[None]) % samples) * (2.0 * math.pi / samples)
    cosine = np.where(inside, np.cos(phase), 0.0) / math.sqrt(samples)
    sine = np.where(inside, -np.sin(phase), 0.0) / math.sqrt(samples)
    upper = np.stack([cosine, sine], axis=2)
    lower = np.stack([-sine, cosine], axis=2)
    return jnp.asarray(np.concatenate([upper, lower], axis=0).astype(np.float32)).astype(jnp.bfloat16)


def row_table(rows):
    sample = jnp.arange(KR, dtype=jnp.int32)[:, None] - KR // 2
    phase = jnp.mod(rows[None, :] * sample, ROWS).astype(jnp.float32) * (2.0 * math.pi / ROWS)
    scale = jnp.where((rows >= 0) & (rows < ROWS), 1.0 / math.sqrt(KR), 0.0)[None, :]
    cosine = jnp.cos(phase) * scale
    sine = jnp.sin(phase) * scale
    upper = jnp.stack([cosine, sine], axis=1)
    lower = jnp.stack([-sine, cosine], axis=1)
    return jnp.concatenate([upper, lower], axis=0).astype(jnp.bfloat16)


def rotation(offsets, samples):
    angle = jnp.mod(offsets[:, None] * (samples[None, :] - KR // 2), ROWS).astype(jnp.float32) * (2.0 * math.pi / ROWS)
    return jnp.cos(angle), jnp.sin(angle)


def plain_body(spectra, offsets):
    own, depth = spectra.shape[:2]
    parts, strips = lax.axis_size("sub"), lax.axis_size("strip")
    wide = COLS // parts + 2
    high = ROWS // strips
    strip = lax.axis_index("strip")
    frames = own * parts
    table = column_table(spectra.shape[2] // 2, parts)
    cosine, sine = rotation(offsets, strip * depth + jnp.arange(depth, dtype=jnp.int32))
    mixed = jnp.einsum("skc,cdpn->dspnk", spectra, table, preferred_element_type=jnp.float32)
    real, imag = mixed[:, :, 0], mixed[:, :, 1]
    cosine, sine = cosine[None, :, None, :], sine[None, :, None, :]
    shifted = jnp.stack([real * cosine - imag * sine, real * sine + imag * cosine], axis=2).astype(jnp.bfloat16)
    held = lax.all_to_all(shifted, "sub", split_axis=0, concat_axis=0, tiled=True)
    held = held.reshape(frames, 2, wide, depth)
    whole = jnp.zeros((frames, 2, wide, strips, depth), jnp.bfloat16)
    for step in range(strips):
        part = held
        if step:
            part = lax.ppermute(held, "strip", [(i, (i + step) % strips) for i in range(strips)])
        source = jnp.mod(strip - step, strips)
        whole = lax.dynamic_update_slice(whole, part[:, :, :, None], (0, 0, 0, source, 0))
    wider = whole.reshape(frames, 2, wide, KR).astype(jnp.float32)
    summed = wider
    for lead in range(1, WIN):
        summed = summed + jnp.roll(wider, -lead, axis=0)
    rows = strip * high + jnp.arange(-1, high + 1, dtype=jnp.int32)
    product = jnp.einsum(
        "fpnk,pkqm->qnfm",
        summed.astype(jnp.bfloat16),
        row_table(rows).reshape(2, KR, 2, high + 2),
        preferred_element_type=jnp.float32,
    )
    log_power = jnp.log(1.0 + product[0] * product[0] + product[1] * product[1])
    total = log_power[:, :, :-2] + log_power[:, :, 1:-1] + log_power[:, :, 2:]
    filtered = (total[:-2] + total[1:-1] + total[2:]) / 9.0
    background = filtered
    for behind in range(1, BG):
        background = background + jnp.roll(filtered, behind, axis=1)
    return jnp.transpose(filtered - background / BG, (2, 0, 1))


LANES = 128
GROUP = 4
MESH = pl.DeviceIdType.MESH


def column_planes(samples):
    phase = (np.arange(COLS)[:, None] * np.arange(samples)[None, :] % samples) * (2.0 * math.pi / samples)
    planes = np.stack([np.cos(phase), -np.sin(phase)]) / math.sqrt(samples)
    return jnp.asarray(planes.astype(np.float32).astype(jnp.bfloat16))


def row_planes(high):
    row = np.concatenate([np.arange(high + LANES - 1), [-1]])
    used = (row <= high)[None, :]
    sample = np.arange(KR)[:, None] - KR // 2
    phase = (row[None, :] * sample % ROWS) * (2.0 * math.pi / ROWS)
    planes = np.stack([np.cos(phase) * used, np.sin(phase) * used]) / math.sqrt(KR)
    return jnp.asarray(planes.astype(np.float32).astype(jnp.bfloat16))


def frame_weights(width, sources, rows):
    frames = 2 * sources
    weights = np.zeros((width, frames, rows), np.float32)
    target = np.arange(frames)

    def place(at, column, frame):
        series = np.where(target == frame, 1.0, 0.0) - np.where((target - frame) % frames < BG, 1.0 / BG, 0.0)
        for near in range(max(column - 1, 0), min(column + 2, width)):
            weights[near, :, at] = series

    for lane in range(2):
        for source in range(sources):
            frame = 2 * source + lane
            for column in range(width):
                place((lane * sources + source) * width + column, column, frame)
            for side in range(2):
                place(2 * sources * width + (lane * sources + source) * 2 + side, (-1, width)[side], frame)
    return jnp.asarray(weights.reshape(width * frames, rows).astype(jnp.bfloat16))


def send_order(layers, group):
    order = [(0, place) for place in range(1, group)]
    half = layers // 2
    turn = [half] + [layer for away in range(half - 1, 0, -1) for layer in (half - away, half + away)]
    return order + [(layer, place) for place in range(group) for layer in turn[1:]] + [(half, place) for place in range(group)]


def product_of(a, b):
    return lax.dot_general(a, b, (((1,), (0,)), ((), ())), preferred_element_type=jnp.float32)


def product_t(a, b):
    return lax.dot_general(a, b, (((1,), (1,)), ((), ())), preferred_element_type=jnp.float32)


def ahead(value, steps):
    return jnp.concatenate([value[steps:], value[:steps]], axis=0)


def kernel(
    parts, strips, offsets_hbm, spectra_hbm, columns_hbm, rows_hbm, weights_hbm, out_ref,
    offsets_ref, spectra, columns, rows, weights, real, imag, edge, main, halo, held, held_halo, lhs, boxed, level,
    load_sem, own_sem, send_sem, recv_sem, pass_sem, got_sem,
):
    me, strip = lax.axis_index("sub"), lax.axis_index("strip")
    width = COLS // parts
    depth = spectra.shape[1]
    samples = spectra.shape[2] // 2
    high = out_ref.shape[2]
    other = 1 - strip

    loads = [
        pltpu.make_async_copy(source, target, load_sem.at[i])
        for i, (source, target) in enumerate(
            [(offsets_hbm, offsets_ref), (spectra_hbm, spectra), (columns_hbm, columns), (rows_hbm, rows), (weights_hbm, weights)]
        )
    ]
    for load in loads[:3]:
        load.start()
    barrier = pltpu.get_barrier_semaphore()
    for away in range(1, parts):
        pl.semaphore_signal(barrier, inc=1, device_id=(lax.rem(me + away, parts), strip), device_id_type=MESH)
    pl.semaphore_signal(barrier, inc=1, device_id=(me, other), device_id_type=MESH)

    loads[0].wait()
    lane = lax.broadcasted_iota(jnp.int32, (1, 2 * depth), 1)
    sample = strip * depth + jnp.where(lane < depth, lane, lane - depth) - KR // 2
    offset = jnp.where(lane < depth, offsets_ref[0], offsets_ref[1])
    angle = jnp.bitwise_and(offset * sample, ROWS - 1).astype(jnp.float32) * (2.0 * math.pi / ROWS)
    cosine, sine = jnp.cos(angle), jnp.sin(angle)
    edge[...] = jnp.zeros_like(edge)
    loads[1].wait()
    loads[2].wait()
    for load in loads[3:]:
        load.start()
    data = spectra[...].reshape(2 * depth, 2 * samples)
    data_re, data_im = data[:, :samples], data[:, samples:]
    step = COLS
    for at in range(0, COLS, step):
        cos_part, sin_part = columns[0, at : at + step], columns[1, at : at + step]
        re = product_t(cos_part, data_re) - product_t(sin_part, data_im)
        im = product_t(sin_part, data_re) + product_t(cos_part, data_im)
        first = at // width
        for part, value, ref in ((0, re * cosine - im * sine, real), (1, re * sine + im * cosine, imag)):
            ref[at : at + step] = value
            blocks = value.reshape(step // width, width, 2 * depth).astype(jnp.bfloat16)
            for own in range(2):
                main[first : first + step // width, own * width : (own + 1) * width, part * depth : (part + 1) * depth] = (
                    blocks[:, :, own * depth : (own + 1) * depth]
                )
    for part, ref in ((0, real), (1, imag)):
        for own in range(2):
            lanes, into = slice(own * depth, (own + 1) * depth), slice(part * depth, (part + 1) * depth)
            for d in range(parts):
                if d > 0:
                    edge[d, 2 * own : 2 * own + 1, into] = ref[d * width - 1 : d * width, lanes]
                if d < parts - 1:
                    edge[d, 2 * own + 1 : 2 * own + 2, into] = ref[(d + 1) * width : (d + 1) * width + 1, lanes]
    halo[...] = edge[:, :4].astype(jnp.bfloat16)

    pl.semaphore_wait(barrier, parts)

    def sends(to, where):
        return [
            pltpu.make_async_remote_copy(
                src_ref=source.at[to], dst_ref=target.at[strip, where], send_sem=send_sem.at[kind, to],
                recv_sem=recv_sem.at[kind, where], device_id=(to, strip), device_id_type=MESH,
            )
            for kind, source, target in ((0, main, held), (1, halo, held_halo))
        ]

    def passes(h, source, own=False):
        return [
            pltpu.make_async_remote_copy(
                src_ref=block.at[source] if own else target.at[h, source], dst_ref=target.at[h, source],
                send_sem=pass_sem.at[kind, source], recv_sem=got_sem.at[kind, source],
                device_id=(me, other), device_id_type=MESH,
            )
            for kind, block, target in ((0, main, held), (1, halo, held_halo))
        ]

    layers = parts // GROUP
    order = send_order(layers, GROUP)

    def device_at(layer, place):
        return lax.rem(me // GROUP + layer, layers) * GROUP + lax.rem(lax.rem(me, GROUP) + place, GROUP)

    def device_from(layer, place):
        return device_at(layers - layer, GROUP - place)

    for away in order:
        for copy in sends(device_at(*away), me):
            copy.start()
    kept = [
        pltpu.make_async_copy(source.at[me], target.at[strip, me], own_sem.at[kind])
        for kind, source, target in ((0, main, held), (1, halo, held_halo))
    ]
    for copy in passes(strip, me, own=True) + kept:
        copy.start()
    for away in order:
        source = device_from(*away)
        for copy in sends(source, source):
            copy.wait_recv()
        for copy in passes(strip, source):
            copy.start()
    top = 2 * parts * width
    odd = lax.rem(lax.broadcasted_iota(jnp.int32, (1, 1, 2 * depth), 2), 2)
    sign = 1.0 - 2.0 * (odd * strip).astype(jnp.float32)
    row_at = lax.broadcasted_iota(jnp.int32, (parts, 8, 2 * depth), 1)
    def window(h):
        block = held[h].astype(jnp.float32) * sign
        first, second = block[:, :width], block[:, width:]
        near = held_halo[h].astype(jnp.float32) * sign
        near = jnp.concatenate([near, jnp.zeros_like(near)], axis=1)
        near_second = jnp.concatenate([pltpu.roll(near[i], 6, 0)[None] for i in range(parts)], axis=0)
        for is_halo, one, two in ((False, first, second), (True, near, near_second)):
            pair = one + two
            double = pair + ahead(pair, 1)
            quad = double + ahead(double, 2)
            for own, frame in ((0, quad), (1, quad - one + ahead(one, WIN // 2))):
                if is_halo:
                    frame = jnp.where(row_at < 2, frame, 0.0)
                    packed = []
                    for group in range(parts // 4):
                        total = frame[4 * group]
                        for j in range(1, 4):
                            total = total + pltpu.roll(frame[4 * group + j], 2 * j, 0)
                        packed.append(total)
                    flat = jnp.concatenate(packed, axis=0).astype(jnp.bfloat16)
                    at, size = top + own * 2 * parts, 2 * parts
                else:
                    flat = frame.reshape(parts * width, 2 * depth).astype(jnp.bfloat16)
                    at, size = own * parts * width, parts * width
                for part in range(2):
                    lhs[at : at + size, pl.ds(pl.multiple_of(part * KR + h * depth, depth), depth)] = flat[
                        :, part * depth : (part + 1) * depth
                    ]

    for copy in kept:
        copy.wait()
    window(strip)
    for away in [(0, 0)] + order:
        for copy in passes(other, device_from(*away)):
            copy.wait_recv()
    window(other)
    loads[3].wait()
    total_rows = top + 4 * parts
    tail = lax.broadcasted_iota(jnp.int32, (1, high + LANES), 1)
    outside = ((tail == high) & (strip == strips - 1)) | ((tail == high + LANES - 1) & (strip == 0))
    inside = jnp.where(outside, 0.0, 1.0)
    chunk = total_rows // 3
    for at in range(0, total_rows, chunk):
        left_re, left_im = lhs[at : at + chunk, :KR], lhs[at : at + chunk, KR:]
        re = product_of(left_re, rows[0]) - product_of(left_im, rows[1])
        im = product_of(left_re, rows[1]) + product_of(left_im, rows[0])
        power = jnp.log(1.0 + re * re + im * im) * inside
        summed = power + pltpu.roll(power, 1, 1) + pltpu.roll(power, high + LANES - 1, 1)
        boxed[at : at + chunk] = summed[:, :high]

    frames = 2 * parts
    block = boxed[:top].reshape(frames, width, high)
    mean = jnp.sum(block, axis=0, keepdims=True) * (1.0 / frames)
    level[:top] = (block - mean).reshape(top, high).astype(jnp.bfloat16)
    near = boxed[top:total_rows].reshape(frames // 4, 8, high)
    mean = jnp.sum(near, axis=0) * (1.0 / frames)
    mean = mean + pltpu.roll(mean, 4, 0)
    mean = mean + pltpu.roll(mean, 2, 0)
    level[top:total_rows] = (near - mean[None]).reshape(total_rows - top, high).astype(jnp.bfloat16)
    level[total_rows:] = jnp.zeros((level.shape[0] - total_rows, high), jnp.bfloat16)
    loads[4].wait()
    for c in range(0, width, 4):
        piece = product_of(weights[c * frames : (c + 4) * frames], level[...])
        out_ref[c : c + 4] = (piece * (1.0 / 9.0)).reshape(4, frames, high)
    for away in order:
        for copy in sends(device_at(*away), me):
            copy.wait_send()
    for away in [(0, 0)] + order:
        for copy in passes(strip, device_from(*away), own=away == (0, 0)):
            copy.wait_send()


def kernel_body(spectra, offsets):
    parts, strips = lax.axis_size("sub"), lax.axis_size("strip")
    own, depth, both = spectra.shape
    width, high = COLS // parts, ROWS // strips
    frames = own * parts
    total_rows = frames * (width + 2)
    padded = -(-total_rows // LANES) * LANES
    bf16, f32 = jnp.bfloat16, jnp.float32
    operands = (offsets, spectra, column_planes(both // 2), row_planes(high), frame_weights(width, parts, padded))
    out = pl.pallas_call(
        functools.partial(kernel, parts, strips),
        out_shape=jax.ShapeDtypeStruct((width, frames, high), f32),
        in_specs=[pl.BlockSpec(memory_space=pltpu.HBM)] * 5,
        out_specs=pl.BlockSpec(memory_space=pltpu.VMEM),
        scratch_shapes=[pltpu.SMEM(offsets.shape, offsets.dtype)]
        + [pltpu.VMEM(operand.shape, operand.dtype) for operand in operands[1:]]
        + [
            pltpu.VMEM((COLS, 2 * depth), f32),
            pltpu.VMEM((COLS, 2 * depth), f32),
            pltpu.VMEM((parts, 8, 2 * depth), f32),
            pltpu.VMEM((parts, 2 * width, 2 * depth), bf16),
            pltpu.VMEM((parts, 4, 2 * depth), bf16),
            pltpu.VMEM((strips, parts, 2 * width, 2 * depth), bf16),
            pltpu.VMEM((strips, parts, 4, 2 * depth), bf16),
            pltpu.VMEM((total_rows, 2 * KR), bf16),
            pltpu.VMEM((total_rows, high), f32),
            pltpu.VMEM((padded, high), bf16),
            pltpu.SemaphoreType.DMA((5,)),
            pltpu.SemaphoreType.DMA((2,)),
            pltpu.SemaphoreType.DMA((2, parts)),
            pltpu.SemaphoreType.DMA((2, parts)),
            pltpu.SemaphoreType.DMA((2, parts)),
            pltpu.SemaphoreType.DMA((2, parts)),
        ],
        compiler_params=pltpu.CompilerParams(collective_id=0, has_side_effects=True, vmem_limit_bytes=48 << 20),
        name="sar",
    )(*(pltpu.with_memory_space_constraint(operand, pltpu.HBM) for operand in operands))
    return jnp.transpose(out, (2, 0, 1))


def fits(mesh):
    parts, strips = mesh.shape["sub"], mesh.shape["strip"]
    return strips == 2 and KR // strips == LANES and COLS % parts == 0 and COLS // parts == 16 and parts % 4 == 0


def body(mesh, spectra, offsets):
    if fits(mesh) and spectra.shape[0] == 2:
        return kernel_body(spectra, offsets)
    return plain_body(spectra, offsets)


def solution(mesh):
    in_specs = (P("sub", "strip", None), P("sub"))
    out_specs = P("strip", "sub", None)
    return jax.shard_map(
        functools.partial(body, mesh), mesh=mesh, in_specs=in_specs, out_specs=out_specs, check_vma=False
    )
```

```python
import functools
import math

import jax
import jax.numpy as jnp
import numpy as np
from jax import lax
from jax.experimental import pallas as pl
from jax.experimental.pallas import tpu as pltpu
from jax.sharding import PartitionSpec as P

KR = 256
ROWS = 1024
COLS = 256
WIN = 8
BG = 16


def column_table(samples, parts):
    wide = COLS // parts + 2
    column = (np.arange(parts) * (wide - 2))[:, None] + np.arange(-1, wide - 1)[None, :]
    inside = (column >= 0) & (column < COLS)
    phase = ((np.arange(samples)[:, None, None] * column[None]) % samples) * (2.0 * math.pi / samples)
    cosine = np.where(inside, np.cos(phase), 0.0) / math.sqrt(samples)
    sine = np.where(inside, -np.sin(phase), 0.0) / math.sqrt(samples)
    upper = np.stack([cosine, sine], axis=2)
    lower = np.stack([-sine, cosine], axis=2)
    return jnp.asarray(np.concatenate([upper, lower], axis=0).astype(np.float32)).astype(jnp.bfloat16)


def row_table(rows):
    sample = jnp.arange(KR, dtype=jnp.int32)[:, None] - KR // 2
    phase = jnp.mod(rows[None, :] * sample, ROWS).astype(jnp.float32) * (2.0 * math.pi / ROWS)
    scale = jnp.where((rows >= 0) & (rows < ROWS), 1.0 / math.sqrt(KR), 0.0)[None, :]
    cosine = jnp.cos(phase) * scale
    sine = jnp.sin(phase) * scale
    upper = jnp.stack([cosine, sine], axis=1)
    lower = jnp.stack([-sine, cosine], axis=1)
    return jnp.concatenate([upper, lower], axis=0).astype(jnp.bfloat16)


def rotation(offsets, samples):
    angle = jnp.mod(offsets[:, None] * (samples[None, :] - KR // 2), ROWS).astype(jnp.float32) * (2.0 * math.pi / ROWS)
    return jnp.cos(angle), jnp.sin(angle)


def plain_body(spectra, offsets):
    own, depth = spectra.shape[:2]
    parts, strips = lax.axis_size("sub"), lax.axis_size("strip")
    wide = COLS // parts + 2
    high = ROWS // strips
    strip = lax.axis_index("strip")
    frames = own * parts
    table = column_table(spectra.shape[2] // 2, parts)
    cosine, sine = rotation(offsets, strip * depth + jnp.arange(depth, dtype=jnp.int32))
    mixed = jnp.einsum("skc,cdpn->dspnk", spectra, table, preferred_element_type=jnp.float32)
    real, imag = mixed[:, :, 0], mixed[:, :, 1]
    cosine, sine = cosine[None, :, None, :], sine[None, :, None, :]
    shifted = jnp.stack([real * cosine - imag * sine, real * sine + imag * cosine], axis=2).astype(jnp.bfloat16)
    held = lax.all_to_all(shifted, "sub", split_axis=0, concat_axis=0, tiled=True)
    held = held.reshape(frames, 2, wide, depth)
    whole = jnp.zeros((frames, 2, wide, strips, depth), jnp.bfloat16)
    for step in range(strips):
        part = held
        if step:
            part = lax.ppermute(held, "strip", [(i, (i + step) % strips) for i in range(strips)])
        source = jnp.mod(strip - step, strips)
        whole = lax.dynamic_update_slice(whole, part[:, :, :, None], (0, 0, 0, source, 0))
    wider = whole.reshape(frames, 2, wide, KR).astype(jnp.float32)
    summed = wider
    for lead in range(1, WIN):
        summed = summed + jnp.roll(wider, -lead, axis=0)
    rows = strip * high + jnp.arange(-1, high + 1, dtype=jnp.int32)
    product = jnp.einsum(
        "fpnk,pkqm->qnfm",
        summed.astype(jnp.bfloat16),
        row_table(rows).reshape(2, KR, 2, high + 2),
        preferred_element_type=jnp.float32,
    )
    log_power = jnp.log(1.0 + product[0] * product[0] + product[1] * product[1])
    total = log_power[:, :, :-2] + log_power[:, :, 1:-1] + log_power[:, :, 2:]
    filtered = (total[:-2] + total[1:-1] + total[2:]) / 9.0
    background = filtered
    for behind in range(1, BG):
        background = background + jnp.roll(filtered, behind, axis=1)
    return jnp.transpose(filtered - background / BG, (2, 0, 1))


LANES = 128
GROUP = 4
MESH = pl.DeviceIdType.MESH


def column_planes(samples):
    phase = (np.arange(COLS)[:, None] * np.arange(samples)[None, :] % samples) * (2.0 * math.pi / samples)
    planes = np.stack([np.cos(phase), -np.sin(phase)]) / math.sqrt(samples)
    return jnp.asarray(planes.astype(np.float32).astype(jnp.bfloat16))


def row_planes(high):
    row = np.concatenate([np.arange(high + LANES - 1), [-1]])
    used = (row <= high)[None, :]
    sample = np.arange(KR)[:, None] - KR // 2
    phase = (row[None, :] * sample % ROWS) * (2.0 * math.pi / ROWS)
    planes = np.stack([np.cos(phase) * used, np.sin(phase) * used]) / math.sqrt(KR)
    return jnp.asarray(planes.astype(np.float32).astype(jnp.bfloat16))


def frame_weights(width, sources, rows):
    frames = 2 * sources
    weights = np.zeros((width, frames, rows), np.float32)
    target = np.arange(frames)

    def place(at, column, frame):
        series = np.where(target == frame, 1.0, 0.0) - np.where((target - frame) % frames < BG, 1.0 / BG, 0.0)
        for near in range(max(column - 1, 0), min(column + 2, width)):
            weights[near, :, at] = series

    for lane in range(2):
        for source in range(sources):
            frame = 2 * source + lane
            for column in range(width):
                place((lane * sources + source) * width + column, column, frame)
            for side in range(2):
                place(2 * sources * width + (lane * sources + source) * 2 + side, (-1, width)[side], frame)
    return jnp.asarray(weights.reshape(width * frames, rows).astype(jnp.bfloat16))


def send_order(layers, group):
    order = [(0, place) for place in range(1, group)]
    half = layers // 2
    turn = [half] + [layer for away in range(half - 1, 0, -1) for layer in (half - away, half + away)]
    return order + [(layer, place) for place in range(group) for layer in turn[1:]] + [(half, place) for place in range(group)]


def product_of(a, b):
    return lax.dot_general(a, b, (((1,), (0,)), ((), ())), preferred_element_type=jnp.float32)


def product_t(a, b):
    return lax.dot_general(a, b, (((1,), (1,)), ((), ())), preferred_element_type=jnp.float32)


def ahead(value, steps):
    return jnp.concatenate([value[steps:], value[:steps]], axis=0)


def kernel(
    parts, strips, offsets_hbm, spectra_hbm, columns_hbm, rows_hbm, weights_hbm, out_ref,
    offsets_ref, spectra, columns, rows, weights, real, imag, edge, main, held, lhs, boxed, level,
    load_sem, own_sem, send_sem, recv_sem, pass_sem, got_sem,
):
    me, strip = lax.axis_index("sub"), lax.axis_index("strip")
    width = COLS // parts
    depth = spectra.shape[1]
    samples = spectra.shape[2] // 2
    high = out_ref.shape[2]
    other = 1 - strip

    loads = [
        pltpu.make_async_copy(source, target, load_sem.at[i])
        for i, (source, target) in enumerate(
            [(offsets_hbm, offsets_ref), (spectra_hbm, spectra), (columns_hbm, columns), (rows_hbm, rows), (weights_hbm, weights)]
        )
    ]
    for load in loads[:3]:
        load.start()
    barrier = pltpu.get_barrier_semaphore()
    for away in range(1, parts):
        pl.semaphore_signal(barrier, inc=1, device_id=(lax.rem(me + away, parts), strip), device_id_type=MESH)
    pl.semaphore_signal(barrier, inc=1, device_id=(me, other), device_id_type=MESH)

    loads[0].wait()
    lane = lax.broadcasted_iota(jnp.int32, (1, 2 * depth), 1)
    sample = strip * depth + jnp.where(lane < depth, lane, lane - depth) - KR // 2
    offset = jnp.where(lane < depth, offsets_ref[0], offsets_ref[1])
    angle = jnp.bitwise_and(offset * sample, ROWS - 1).astype(jnp.float32) * (2.0 * math.pi / ROWS)
    cosine, sine = jnp.cos(angle), jnp.sin(angle)
    edge[...] = jnp.zeros_like(edge)
    loads[1].wait()
    loads[2].wait()
    for load in loads[3:]:
        load.start()
    data = spectra[...].reshape(2 * depth, 2 * samples)
    data_re, data_im = data[:, :samples], data[:, samples:]
    step = COLS
    for at in range(0, COLS, step):
        cos_part, sin_part = columns[0, at : at + step], columns[1, at : at + step]
        re = product_t(cos_part, data_re) - product_t(sin_part, data_im)
        im = product_t(sin_part, data_re) + product_t(cos_part, data_im)
        first = at // width
        for part, value, ref in ((0, re * cosine - im * sine, real), (1, re * sine + im * cosine, imag)):
            ref[at : at + step] = value
            blocks = value.reshape(step // width, width // 4, 4, 2 * depth).astype(jnp.bfloat16)
            for own in range(2):
                main[
                    first : first + step // width, own * width // 4 : (own + 1) * width // 4, :, part * depth : (part + 1) * depth
                ] = blocks[:, :, :, own * depth : (own + 1) * depth]
    for part, ref in ((0, real), (1, imag)):
        for own in range(2):
            lanes, into = slice(own * depth, (own + 1) * depth), slice(part * depth, (part + 1) * depth)
            for d in range(parts):
                if d > 0:
                    edge[d, 2 * own : 2 * own + 1, into] = ref[d * width - 1 : d * width, lanes]
                if d < parts - 1:
                    edge[d, 2 * own + 1 : 2 * own + 2, into] = ref[(d + 1) * width : (d + 1) * width + 1, lanes]
    main[:, 2 * width // 4] = edge[:, :4].astype(jnp.bfloat16)

    pl.semaphore_wait(barrier, parts)

    def sends(to, where):
        return [
            pltpu.make_async_remote_copy(
                src_ref=source.at[to], dst_ref=target.at[strip, where], send_sem=send_sem.at[kind, to],
                recv_sem=recv_sem.at[kind, where], device_id=(to, strip), device_id_type=MESH,
            )
            for kind, source, target in ((0, main, held),)
        ]

    def passes(h, source, own=False):
        return [
            pltpu.make_async_remote_copy(
                src_ref=block.at[source] if own else target.at[h, source], dst_ref=target.at[h, source],
                send_sem=pass_sem.at[kind, source], recv_sem=got_sem.at[kind, source],
                device_id=(me, other), device_id_type=MESH,
            )
            for kind, block, target in ((0, main, held),)
        ]

    layers = parts // GROUP
    order = send_order(layers, GROUP)

    def device_at(layer, place):
        return lax.rem(me // GROUP + layer, layers) * GROUP + lax.rem(lax.rem(me, GROUP) + place, GROUP)

    def device_from(layer, place):
        return device_at(layers - layer, GROUP - place)

    for away in order:
        for copy in sends(device_at(*away), me):
            copy.start()
    kept = [
        pltpu.make_async_copy(source.at[me], target.at[strip, me], own_sem.at[kind])
        for kind, source, target in ((0, main, held),)
    ]
    for copy in passes(strip, me, own=True) + kept:
        copy.start()
    for away in order:
        source = device_from(*away)
        for copy in sends(source, source):
            copy.wait_recv()
        for copy in passes(strip, source):
            copy.start()
    top = 2 * parts * width
    odd = lax.rem(lax.broadcasted_iota(jnp.int32, (1, 1, 2 * depth), 2), 2)
    sign = 1.0 - 2.0 * (odd * strip).astype(jnp.float32)
    row_at = lax.broadcasted_iota(jnp.int32, (parts, 8, 2 * depth), 1)
    def window(h):
        whole = held[h].astype(jnp.float32) * sign[None]
        block = whole[:, : 2 * width // 4].reshape(parts, 2 * width, 2 * depth)
        first, second = block[:, :width], block[:, width:]
        near = whole[:, 2 * width // 4]
        near = jnp.concatenate([near, jnp.zeros_like(near)], axis=1)
        near_second = jnp.concatenate([pltpu.roll(near[i], 6, 0)[None] for i in range(parts)], axis=0)
        for is_halo, one, two in ((False, first, second), (True, near, near_second)):
            pair = one + two
            double = pair + ahead(pair, 1)
            quad = double + ahead(double, 2)
            for own, frame in ((0, quad), (1, quad - one + ahead(one, WIN // 2))):
                if is_halo:
                    frame = jnp.where(row_at < 2, frame, 0.0)
                    packed = []
                    for group in range(parts // 4):
                        total = frame[4 * group]
                        for j in range(1, 4):
                            total = total + pltpu.roll(frame[4 * group + j], 2 * j, 0)
                        packed.append(total)
                    flat = jnp.concatenate(packed, axis=0).astype(jnp.bfloat16)
                    at, size = top + own * 2 * parts, 2 * parts
                else:
                    flat = frame.reshape(parts * width, 2 * depth).astype(jnp.bfloat16)
                    at, size = own * parts * width, parts * width
                for part in range(2):
                    lhs[at : at + size, pl.ds(pl.multiple_of(part * KR + h * depth, depth), depth)] = flat[
                        :, part * depth : (part + 1) * depth
                    ]

    for copy in kept:
        copy.wait()
    window(strip)
    for away in [(0, 0)] + order:
        for copy in passes(other, device_from(*away)):
            copy.wait_recv()
    window(other)
    loads[3].wait()
    total_rows = top + 4 * parts
    tail = lax.broadcasted_iota(jnp.int32, (1, high + LANES), 1)
    outside = ((tail == high) & (strip == strips - 1)) | ((tail == high + LANES - 1) & (strip == 0))
    inside = jnp.where(outside, 0.0, 1.0)
    chunk = total_rows // 3
    for at in range(0, total_rows, chunk):
        left_re, left_im = lhs[at : at + chunk, :KR], lhs[at : at + chunk, KR:]
        re = product_of(left_re, rows[0]) - product_of(left_im, rows[1])
        im = product_of(left_re, rows[1]) + product_of(left_im, rows[0])
        power = jnp.log(1.0 + re * re + im * im) * inside
        summed = power + pltpu.roll(power, 1, 1) + pltpu.roll(power, high + LANES - 1, 1)
        boxed[at : at + chunk] = summed[:, :high]

    frames = 2 * parts
    block = boxed[:top].reshape(frames, width, high)
    mean = jnp.sum(block, axis=0, keepdims=True) * (1.0 / frames)
    level[:top] = (block - mean).reshape(top, high).astype(jnp.bfloat16)
    near = boxed[top:total_rows].reshape(frames // 4, 8, high)
    mean = jnp.sum(near, axis=0) * (1.0 / frames)
    mean = mean + pltpu.roll(mean, 4, 0)
    mean = mean + pltpu.roll(mean, 2, 0)
    level[top:total_rows] = (near - mean[None]).reshape(total_rows - top, high).astype(jnp.bfloat16)
    level[total_rows:] = jnp.zeros((level.shape[0] - total_rows, high), jnp.bfloat16)
    loads[4].wait()
    for c in range(0, width, 4):
        piece = product_of(weights[c * frames : (c + 4) * frames], level[...])
        out_ref[c : c + 4] = (piece * (1.0 / 9.0)).reshape(4, frames, high)
    for away in order:
        for copy in sends(device_at(*away), me):
            copy.wait_send()
    for away in [(0, 0)] + order:
        for copy in passes(strip, device_from(*away), own=away == (0, 0)):
            copy.wait_send()


def kernel_body(spectra, offsets):
    parts, strips = lax.axis_size("sub"), lax.axis_size("strip")
    own, depth, both = spectra.shape
    width, high = COLS // parts, ROWS // strips
    frames = own * parts
    total_rows = frames * (width + 2)
    padded = -(-total_rows // LANES) * LANES
    bf16, f32 = jnp.bfloat16, jnp.float32
    operands = (offsets, spectra, column_planes(both // 2), row_planes(high), frame_weights(width, parts, padded))
    out = pl.pallas_call(
        functools.partial(kernel, parts, strips),
        out_shape=jax.ShapeDtypeStruct((width, frames, high), f32),
        in_specs=[pl.BlockSpec(memory_space=pltpu.HBM)] * 5,
        out_specs=pl.BlockSpec(memory_space=pltpu.VMEM),
        scratch_shapes=[pltpu.SMEM(offsets.shape, offsets.dtype)]
        + [pltpu.VMEM(operand.shape, operand.dtype) for operand in operands[1:]]
        + [
            pltpu.VMEM((COLS, 2 * depth), f32),
            pltpu.VMEM((COLS, 2 * depth), f32),
            pltpu.VMEM((parts, 8, 2 * depth), f32),
            pltpu.VMEM((parts, 2 * width // 4 + 1, 4, 2 * depth), bf16),
            pltpu.VMEM((strips, parts, 2 * width // 4 + 1, 4, 2 * depth), bf16),
            pltpu.VMEM((total_rows, 2 * KR), bf16),
            pltpu.VMEM((total_rows, high), f32),
            pltpu.VMEM((padded, high), bf16),
            pltpu.SemaphoreType.DMA((5,)),
            pltpu.SemaphoreType.DMA((1,)),
            pltpu.SemaphoreType.DMA((1, parts)),
            pltpu.SemaphoreType.DMA((1, parts)),
            pltpu.SemaphoreType.DMA((1, parts)),
            pltpu.SemaphoreType.DMA((1, parts)),
        ],
        compiler_params=pltpu.CompilerParams(collective_id=0, has_side_effects=True, vmem_limit_bytes=48 << 20),
        name="sar",
    )(*(pltpu.with_memory_space_constraint(operand, pltpu.HBM) for operand in operands))
    return jnp.transpose(out, (2, 0, 1))


def fits(mesh):
    parts, strips = mesh.shape["sub"], mesh.shape["strip"]
    return strips == 2 and KR // strips == LANES and COLS % parts == 0 and COLS // parts == 16 and parts % 4 == 0


def body(mesh, spectra, offsets):
    if fits(mesh) and spectra.shape[0] == 2:
        return kernel_body(spectra, offsets)
    return plain_body(spectra, offsets)


def solution(mesh):
    in_specs = (P("sub", "strip", None), P("sub"))
    out_specs = P("strip", "sub", None)
    return jax.shard_map(
        functools.partial(body, mesh), mesh=mesh, in_specs=in_specs, out_specs=out_specs, check_vma=False
    )
```
